512 devices in a mesh: ctx: 32 (over z, x_hi, core), head: 16 (over x_lo, y).
Axes of the slice: x: 4 (x_hi: 2, x_lo: 2; x = x_hi * 2 + x_lo), y: 8, z: 8, core: 2. Of those that a mesh axis runs over, the one named last changes fastest.
Arguments:
- q_nope: bfloat16 [4096, 8192], P('ctx', 'head'), may hold values from -6 to 6
- q_rope: bfloat16 [4096, 4096], P('ctx', 'head'), may hold values from -9 to 9
- latent: bfloat16 [32, 128, 512], P('ctx'), may hold values from -6 to 6
- key_rope: bfloat16 [32, 64, 128], P('ctx'), may hold values from -9 to 9
- chosen: int32 [32, 20], P('ctx'), may hold values from 0 to 31, as said below
- w_uk: bfloat16 [64, 128, 512], P('head'), may hold values from -0.5 to 0.5
- w_uv: bfloat16 [64, 512, 128], P('head'), may hold values from -1.5 to 1.5
- w_out: bfloat16 [8192, 3584], P('head'), may hold values from -0.09375 to 0.09375
Outputs:
- mixed: bfloat16 [4096, 3584], P('ctx', 'head')
The draws below stay inside these ranges and needn't reach their ends.
Inputs may be any that keep to these rules, and one draw needn't show every extreme that they name: `chosen`: row b lists key blocks numbered 0 to b; b itself always appears, an entry may repeat and then counts once, and row 31 lists 20 different blocks.
All inputs are finite; a program needn't handle non-finite values.
Results may differ from the reference program's by a relative error of at most 0.019.
Values may be sent and summed in bfloat16 or wider, within the bound.
A program may use at most 64 MiB of HBM per device.

```python
import jax
import jax.numpy as jnp
from jax import lax

LAT = 512
ROPE = 64
QK_NOPE = 128
VHEAD = 128
DW = 3584
BLOCK = 128
NBLK = 32
TOKENS = 4096
H = 64
MOST = 20


def draw_key_rope(key, part):
    noise_key = jax.random.fold_in(key, 11)
    values = jnp.clip(jax.random.normal(noise_key, (NBLK, ROPE, BLOCK), jnp.float32), -4.5, 4.5)
    return values.astype(jnp.bfloat16)


def draw_q_rope(key, part):
    noise_key = jax.random.fold_in(key, 13)
    values = jnp.clip(jax.random.normal(noise_key, (TOKENS, H, ROPE), jnp.float32), -4.5, 4.5)
    return values.reshape(TOKENS, H * ROPE).astype(jnp.bfloat16)


def draw_chosen(key, part):
    count_key = jax.random.fold_in(key, 17)
    order_key = jax.random.fold_in(key, 19)
    block_ids = jnp.arange(NBLK, dtype=jnp.int32)
    available = jnp.minimum(block_ids + 1, MOST)
    pick_count = jax.random.randint(count_key, (NBLK,), 0, available) + 1
    pick_count = pick_count.at[NBLK - 1].set(MOST)
    priority = jax.random.randint(order_key, (NBLK, NBLK), 0, 1 << 20) * NBLK + block_ids[None, :]
    priority = jnp.where(block_ids[None, :] > block_ids[:, None], 1 << 30, priority)
    priority = jnp.where(block_ids[None, :] == block_ids[:, None], -1, priority)
    ranking = jnp.argsort(priority, axis=1, stable=True).astype(jnp.int32)[:, :MOST]
    slot_ids = jnp.arange(MOST, dtype=jnp.int32)
    lists = jnp.where(slot_ids[None, :] < pick_count[:, None], ranking, block_ids[:, None])
    return lists.astype(jnp.int32)


def with_spikes(values, rng, source, target, parts, factor):
    owner, partner = [(jnp.arange(values.shape[dim]) // (values.shape[dim] // parts)).reshape([-1 if axis == dim else 1 for axis in range(values.ndim)]) for dim in (source, target)]
    chosen = jax.random.permutation(rng, parts)[partner]
    strong = (owner == chosen) | (owner == (partner + parts // 2) % parts)
    return jnp.where(strong, factor * values, values)


def steps_of(own_key, dims, cuts, low, top_value):
    gain = 1.0
    for dim, shards_of in cuts:
        heights = jax.random.uniform(jax.random.fold_in(jax.random.fold_in(own_key, 6), dim), (shards_of,), jnp.float32, low / len(cuts), top_value / len(cuts))
        gain = gain * jnp.repeat(jnp.exp(heights), dims[dim] // shards_of).reshape((-1,) + (1,) * (len(dims) - 1 - dim))
    return gain


def normal_values(own_key, shape, deviation, most, split=(), kind=jnp.bfloat16):
    gain = steps_of(own_key, shape, split, -0.22, 0.18) if split else 1.0
    values = jax.random.normal(own_key, shape, jnp.float32) * deviation * gain
    return jnp.minimum(jnp.maximum(values, -most), most).astype(kind)


def gaussian_with(key, dims, spread, bound, shards, heavy, held_as=jnp.bfloat16):
    values = spread * jax.random.normal(key, dims, jnp.float32)
    if shards:
        values = values * steps_of(key, dims, shards, -0.22, 0.18)
    return jnp.clip(with_spikes(values, jax.random.fold_in(key, 3), *heavy), -bound, bound).astype(held_as)


def setup_inputs(seed: int = 0) -> dict:
    seeds = jax.random.split(jax.random.key(seed), 9)
    q_nope = normal_values(seeds[0], (TOKENS, H * QK_NOPE), 1.0, 6.0, ((0, 32), (1, 16)))
    q_rope = draw_q_rope(jax.random.fold_in(seeds[8], 71), 0)
    latent = normal_values(seeds[2], (NBLK, BLOCK, LAT), 1.0, 6.0, ((0, 32),))
    key_rope = draw_key_rope(jax.random.fold_in(seeds[8], 71), 0)
    chosen = draw_chosen(jax.random.fold_in(seeds[8], 71), 0)
    w_uk = normal_values(seeds[5], (H, QK_NOPE, LAT), QK_NOPE ** -0.5, 0.5, ((0, 16),))
    w_uv = normal_values(seeds[6], (H, LAT, VHEAD), (LAT // 32) ** -0.5, 1.5, ((0, 16),))
    w_out = gaussian_with(seeds[7], (H * VHEAD, DW), (H * VHEAD) ** -0.5, 0.09375, ((0, 16),), (0, 1, 16, 2.0))
    return dict(q_nope=q_nope, q_rope=q_rope, latent=latent, key_rope=key_rope, chosen=chosen, w_uk=w_uk, w_uv=w_uv, w_out=w_out)


MASKED_SCORE = -1e30


def rounded(values):
    narrow = lax.optimization_barrier(values.astype(jnp.bfloat16))
    return narrow.astype(jnp.float32)


def reference(q_nope, q_rope, latent, key_rope, chosen, w_uk, w_uv, w_out):
    score_scale = (QK_NOPE + ROPE) ** -0.5
    head_count = w_uk.shape[0]
    nope_parts = q_nope.astype(jnp.float32).reshape(NBLK, BLOCK, head_count, QK_NOPE)
    rope_parts = q_rope.astype(jnp.float32).reshape(NBLK, BLOCK, head_count, ROPE)
    key_up = w_uk.astype(jnp.float32)
    value_up = w_uv.astype(jnp.float32)
    latent_wide = latent.astype(jnp.float32)
    rope_wide = key_rope.astype(jnp.float32)
    row_ids = jnp.arange(BLOCK, dtype=jnp.int32)
    slot_ids = jnp.arange(MOST, dtype=jnp.int32)

    def one_block(inputs):
        block_id, nope_block, rope_block, key_lists = inputs
        query_lat = rounded(jnp.einsum('ihn,hnl->hil', nope_block, key_up))
        key_latent = latent_wide[key_lists].reshape(MOST * BLOCK, LAT)
        key_columns = jnp.transpose(rope_wide[key_lists], (1, 0, 2)).reshape(ROPE, MOST * BLOCK)
        scores = jnp.einsum('hil,jl->hij', query_lat, key_latent)
        scores = (scores + jnp.einsum('ihr,rj->hij', rope_block, key_columns)) * score_scale
        earlier = slot_ids[:, None] > slot_ids[None, :]
        repeated = jnp.any((key_lists[:, None] == key_lists[None, :]) & earlier, axis=1)
        own_block = key_lists == block_id
        causal = row_ids[None, None, :] <= row_ids[:, None, None]
        allowed = jnp.logical_not(repeated)[None, :, None] & (jnp.logical_not(own_block)[None, :, None] | causal)
        allowed = allowed.reshape(BLOCK, MOST * BLOCK)[None]
        scores = jnp.where(allowed, scores, MASKED_SCORE)
        row_max = jnp.max(scores, axis=-1, keepdims=True)
        exponent = jnp.where(allowed, jnp.exp(scores - row_max), 0.0)
        row_sum = jnp.sum(exponent, axis=-1, keepdims=True)
        mixed_latent = rounded(jnp.einsum('hij,jl->hil', rounded(exponent), key_latent) / row_sum)
        head_values = jnp.einsum('hil,hlv->ihv', mixed_latent, value_up)
        return head_values.astype(jnp.bfloat16).reshape(BLOCK, head_count * VHEAD)

    block_ids = jnp.arange(NBLK, dtype=jnp.int32)
    value_rows = lax.map(one_block, (block_ids, nope_parts, rope_parts, chosen))
    value_rows = value_rows.reshape(TOKENS, head_count * VHEAD)
    return jnp.dot(value_rows, w_out, preferred_element_type=jnp.float32).astype(jnp.bfloat16)
```

```python
import math

import jax
import jax.numpy as jnp
from jax import lax
from jax.experimental import pallas as pl
from jax.experimental.pallas import tpu as pltpu
from jax.sharding import PartitionSpec as P

LAT = 512
ROPE = 64
QK_NOPE = 128
VHEAD = 128
BLOCK = 128
ROWS = 144
THIRD = 48
PIECES = 3
MASKED = -1e30
MESH = pl.DeviceIdType.MESH


def gather_attend(
    heads,
    planes,
    ys,
    q_nope,
    q_rope,
    latent,
    key_rope,
    chosen,
    w_uk,
    w_uv,
    values,
    kv,
    qn_buf,
    qr_buf,
    wuk_buf,
    wuv_buf,
    q_lat,
    q_rot,
    bias,
    row_max,
    row_sum,
    acc,
    load_sem,
    x_send,
    x_recv,
    own_send,
    own_recv,
    xp_send,
    xp_recv,
    z_send,
    z_recv,
    y_send,
    y_recv,
    zp_send,
    zp_recv,
    yp_send,
    yp_recv,
):
    ci = lax.axis_index("ctx")
    hi = lax.axis_index("head")
    z, xh, core = ci // 4, (ci // 2) % 2, ci % 2
    xl, y = hi // ys, hi % ys
    color = y % 2

    def ctx_at(zz):
        return lax.rem(zz + planes, planes) * 4 + xh * 2 + core

    def head_at(yy):
        return xl * ys + lax.rem(yy + ys, ys)

    partner = (z * 4 + xh * 2 + (1 - core), hi)
    across = (z * 4 + (1 - xh) * 2 + core, (1 - xl) * ys + y)
    z_next, z_prev = (ctx_at(z + 1), hi), (ctx_at(z - 1), hi)
    y_next, y_prev = (ci, head_at(y + 1)), (ci, head_at(y - 1))
    toward_z = (z_next, z_prev)
    toward_y = (y_next, y_prev)

    loads = [pltpu.make_async_copy(latent.at[0], kv.at[ci, 0:BLOCK, :], load_sem.at[0])]
    for i in range(4):
        loads.append(
            pltpu.make_async_copy(
                key_rope.at[0, 16 * i : 16 * i + 16, :],
                kv.at[ci, BLOCK:ROWS, 128 * i : 128 * i + 128],
                load_sem.at[1 + i],
            )
        )
    for i, (src, dst) in enumerate(
        ((q_nope, qn_buf), (w_uk, wuk_buf), (q_rope, qr_buf), (w_uv, wuv_buf))
    ):
        loads.append(pltpu.make_async_copy(src, dst, load_sem.at[5 + i]))
    for copy in loads:
        copy.start()

    barrier = pltpu.get_barrier_semaphore()
    for device in (partner, across, z_next, z_prev, y_next, y_prev):
        pl.semaphore_signal(barrier, inc=1, device_id=device, device_id_type=MESH)
    pl.semaphore_wait(barrier, 6)

    def part(block, p):
        return kv.at[block, THIRD * p : THIRD * (p + 1), :]

    def send(block, p, send_sem, recv_sem, device):
        return pltpu.make_async_remote_copy(
            part(block, p), part(block, p), send_sem, recv_sem, device_id=device, device_id_type=MESH
        )

    def plane_of(d, hop):
        return lax.rem(z + planes - hop, planes) if d == 0 else lax.rem(z + hop, planes)

    def mine(plane):
        return plane * 4 + color * 2 + core

    def other(plane):
        return plane * 4 + (1 - color) * 2 + core

    def z_copy(d, hop, p):
        return send(mine(plane_of(d, hop - 1)), p, z_send.at[d, hop - 1, p], z_recv.at[d, hop - 1, p], toward_z[d])

    def y_copy(d, hop, p):
        return send(mine(plane_of(d, hop)), p, y_send.at[d, hop - 1, p], y_recv.at[d, hop - 1, p], toward_y[d])

    def y_arrival(d, hop, p):
        return send(other(plane_of(d, hop)), p, y_send.at[d, hop - 1, p], y_recv.at[d, hop - 1, p], toward_y[d])

    def zp_copy(d, hop, p):
        return send(mine(plane_of(d, hop)), p, zp_send.at[d, hop - 1, p], zp_recv.at[d, hop - 1, p], partner)

    def yp_copy(d, hop, p):
        return send(other(plane_of(d, hop)), p, yp_send.at[d, hop - 1, p], yp_recv.at[d, hop - 1, p], partner)

    def carried(d, hop, p):
        return hop < 4 or (p < 2 if d == 0 else p == 2)

    for copy in loads[:5]:
        copy.wait()
    across_block = z * 4 + (1 - xh) * 2 + core
    x_copies = [send(ci, p, x_send.at[p], x_recv.at[p], across) for p in range(PIECES)]
    for copy in x_copies:
        copy.start()
    own_copy = pltpu.make_async_remote_copy(
        kv.at[ci], kv.at[ci], own_send.at[0], own_recv.at[0], device_id=partner, device_id_type=MESH
    )
    own_copy.start()

    @pl.when(xh == color)
    def _():
        for p in range(PIECES):
            for d in range(2):
                z_copy(d, 1, p).start()

    block_ids = lax.broadcasted_iota(jnp.int32, (planes * 4, BLOCK), 0)
    listed = block_ids < 0
    for j in range(chosen.shape[1]):
        listed = jnp.logical_or(listed, block_ids == chosen[0, j])
    bias[...] = jnp.where(listed, 0.0, MASKED)
    row_max[...] = jnp.full_like(row_max, MASKED)
    row_sum[...] = jnp.zeros_like(row_sum)
    acc[...] = jnp.zeros_like(acc)

    xp_copies = [send(across_block, p, xp_send.at[p], xp_recv.at[p], partner) for p in range(PIECES)]
    for p in range(PIECES):
        x_copies[p].wait_recv()
        xp_copies[p].start()

        @pl.when(xh != color)
        def _():
            for d in range(2):
                z_copy(d, 1, p).start()

    for copy in loads[5:8]:
        copy.wait()
    for h in range(heads):
        rows = slice(BLOCK * h, BLOCK * (h + 1))
        q_lat[rows, :] = jnp.dot(
            qn_buf[:, QK_NOPE * h : QK_NOPE * (h + 1)], wuk_buf[h], preferred_element_type=jnp.float32
        ).astype(jnp.bfloat16)
        q_rot[rows, :] = qr_buf[:, ROPE * h : ROPE * (h + 1)]

    scale = (QK_NOPE + ROPE) ** -0.5 * math.log2(math.e)
    half = heads * BLOCK // 2

    def attend(plane, r, own):
        rows = slice(half * r, half * (r + 1))
        first = plane * 4
        keys = jnp.concatenate([kv[first + i, 0:BLOCK, :] for i in range(4)], axis=0)
        rotary = jnp.concatenate(
            [
                jnp.concatenate(
                    [kv[first + i, BLOCK:ROWS, 128 * j : 128 * (j + 1)] for j in range(4)], axis=0
                )
                for i in range(4)
            ],
            axis=1,
        )
        scores = lax.dot_general(
            q_lat[rows, :], keys, (((1,), (1,)), ((), ())), preferred_element_type=jnp.float32
        )
        scores = scores + jnp.dot(q_rot[rows, :], rotary, preferred_element_type=jnp.float32)
        hidden = jnp.concatenate([bias[pl.ds(first + i, 1), :] for i in range(4)], axis=1)
        scores = scores * scale + hidden
        if own:
            t_ids = lax.broadcasted_iota(jnp.int32, scores.shape, 0) % BLOCK
            col_ids = lax.broadcasted_iota(jnp.int32, scores.shape, 1)
            u_ids = col_ids - (ci % 4) * BLOCK
            later = (u_ids > t_ids) & (u_ids < BLOCK)
            scores = jnp.where(later, MASKED, scores)
        old_max = row_max[rows, :]
        new_max = jnp.maximum(old_max, jnp.max(scores, axis=1, keepdims=True))
        factor = jnp.exp2(old_max - new_max)
        wide = jnp.concatenate([new_max] * 4, axis=1)
        exponent = jnp.exp2(scores - wide)
        total = exponent[:, 0:128] + exponent[:, 128:256] + exponent[:, 256:384] + exponent[:, 384:512]
        row_max[rows, :] = new_max
        row_sum[rows, :] = row_sum[rows, :] * factor + total
        acc[rows, :] = acc[rows, :] * jnp.concatenate([factor] * 4, axis=1) + jnp.dot(
            exponent.astype(jnp.bfloat16), keys, preferred_element_type=jnp.float32
        )

    def z_arrive(d, hop, p):
        z_copy(d, hop, p).wait_recv()

    own_copy.wait_recv()
    for p in range(PIECES):
        xp_copies[p].wait_recv()

    def step(hop, c):
        for p in range(PIECES):
            for d in range(2):

                @pl.when((hop < 4) | ((hop == 4) & (p < 2 if d == 0 else p == 2)))
                def _():
                    z_copy(d, hop, p).wait_recv()

                @pl.when((hop < 3) | ((hop == 3) & (p < 2 if d == 0 else p == 2)))
                def _():
                    z_copy(d, hop + 1, p).start()

                @pl.when((hop < 4) | ((hop == 4) & (p < 2 if d == 0 else p == 2)))
                def _():
                    y_copy(d, hop, p).start()
                    zp_copy(d, hop, p).start()

            before = hop - 1
            for d in range(2):

                @pl.when((before >= 1) & ((before < 4) | ((before == 4) & (p < 2 if d == 0 else p == 2))))
                def _():
                    y_arrival(d, before, p).wait_recv()
                    yp_copy(d, before, p).start()

            if p == 0:

                @pl.when(hop == 1)
                def _():
                    for r in range(2):
                        attend(z, r, True)

            ready = hop - 2
            if p > 0:
                d = p - 1

                @pl.when((ready >= 1) & (ready < 4))
                def _():
                    for q in range(PIECES):
                        zp_copy(d, ready, q).wait_recv()
                        yp_copy(d, ready, q).wait_recv()
                    for r in range(2):
                        attend(plane_of(d, ready), r, False)

        return c

    lax.fori_loop(1, 6, step, 0)
    for d in range(2):
        for p in range(PIECES):
            if carried(d, 4, p):
                zp_copy(d, 4, p).wait_recv()
                yp_copy(d, 4, p).wait_recv()
    for r in range(2):
        attend(plane_of(0, 4), r, False)

    loads[8].wait()
    for h in range(heads):
        rows = slice(BLOCK * h, BLOCK * (h + 1))
        denominator = jnp.sum(row_sum[rows, :], axis=1, keepdims=True)
        mix = (acc[rows, :] / denominator).astype(jnp.bfloat16)
        values[:, VHEAD * h : VHEAD * (h + 1)] = jnp.dot(
            mix, wuv_buf[h], preferred_element_type=jnp.float32
        ).astype(jnp.bfloat16)

    for copy in x_copies + xp_copies + [own_copy]:
        copy.wait_send()
    for d in range(2):
        for hop in range(1, 5):
            for p in range(PIECES):
                if carried(d, hop, p):
                    z_copy(d, hop, p).wait_send()
                    y_copy(d, hop, p).wait_send()
                    zp_copy(d, hop, p).wait_send()
                    yp_copy(d, hop, p).wait_send()


def solution(mesh):
    planes = mesh.shape["ctx"] // 4
    ys = mesh.shape["head"] // 2

    def on_device(q_nope, q_rope, latent, key_rope, chosen, w_uk, w_uv, w_out):
        heads = w_uk.shape[0]
        tokens = q_nope.shape[0]
        rows = heads * tokens
        anywhere = pl.BlockSpec(memory_space=pl.ANY)
        dma = pltpu.SemaphoreType.DMA

        def kernel(*refs):
            gather_attend(heads, planes, ys, *refs)

        values = pl.pallas_call(
            kernel,
            out_shape=jax.ShapeDtypeStruct((tokens, heads * VHEAD), jnp.bfloat16),
            in_specs=[
                anywhere,
                anywhere,
                anywhere,
                anywhere,
                pl.BlockSpec(memory_space=pltpu.SMEM),
                anywhere,
                anywhere,
            ],
            out_specs=pl.BlockSpec(memory_space=pltpu.VMEM),
            scratch_shapes=[
                pltpu.VMEM((planes * 4, ROWS, LAT), jnp.bfloat16),
                pltpu.VMEM(q_nope.shape, jnp.bfloat16),
                pltpu.VMEM(q_rope.shape, jnp.bfloat16),
                pltpu.VMEM(w_uk.shape, jnp.bfloat16),
                pltpu.VMEM(w_uv.shape, jnp.bfloat16),
                pltpu.VMEM((rows, LAT), jnp.bfloat16),
                pltpu.VMEM((rows, ROPE), jnp.bfloat16),
                pltpu.VMEM((planes * 4, BLOCK), jnp.float32),
                pltpu.VMEM((rows, 128), jnp.float32),
                pltpu.VMEM((rows, 128), jnp.float32),
                pltpu.VMEM((rows, LAT), jnp.float32),
                dma((9,)),
                dma((3,)),
                dma((3,)),
                dma((1,)),
                dma((1,)),
                dma((3,)),
                dma((3,)),
            ]
            + [dma((2, 4, 3))] * 8,
            compiler_params=pltpu.CompilerParams(
                collective_id=0, has_side_effects=True, vmem_limit_bytes=48 << 20
            ),
        )(q_nope, q_rope, latent, key_rope, chosen, w_uk, w_uv)
        partial = jnp.dot(values, w_out, preferred_element_type=jnp.float32)
        return lax.psum_scatter(
            partial.astype(jnp.bfloat16), "head", scatter_dimension=1, tiled=True
        )

    return jax.shard_map(
        on_device,
        mesh=mesh,
        in_specs=(
            P("ctx", "head"),
            P("ctx", "head"),
            P("ctx", None, None),
            P("ctx", None, None),
            P("ctx", None),
            P("head", None, None),
            P("head", None, None),
            P("head", None),
        ),
        out_specs=P("ctx", "head"),
        check_vma=False,
    )
```

```python
import math

import jax
import jax.numpy as jnp
from jax import lax
from jax.experimental import pallas as pl
from jax.experimental.pallas import tpu as pltpu
from jax.sharding import PartitionSpec as P

LAT = 512
ROPE = 64
QK_NOPE = 128
VHEAD = 128
BLOCK = 128
ROWS = 144
THIRD = 48
PIECES = 3
MASKED = -1e30
MESH = pl.DeviceIdType.MESH


def gather_attend(
    heads,
    planes,
    ys,
    q_nope,
    q_rope,
    latent,
    key_rope,
    chosen,
    w_uk,
    w_uv,
    w_out,
    out,
    kv,
    qn_buf,
    qr_buf,
    wuk_buf,
    wuv_buf,
    q_lat,
    q_rot,
    bias,
    row_max,
    row_sum,
    acc,
    load_sem,
    x_send,
    x_recv,
    own_send,
    own_recv,
    xp_send,
    xp_recv,
    z_send,
    z_recv,
    y_send,
    y_recv,
    zp_send,
    zp_recv,
    yp_send,
    yp_recv,
    w_mine,
    w_peer,
    w_turned,
    values,
    v_peer,
    piece,
    staged,
    landed,
    w_send,
    w_recv,
    v_send,
    v_recv,
    r_send,
    r_recv,
):
    ci = lax.axis_index("ctx")
    hi = lax.axis_index("head")
    z, xh, core = ci // 4, (ci // 2) % 2, ci % 2
    xl, y = hi // ys, hi % ys
    color = y % 2

    def ctx_at(zz):
        return lax.rem(zz + planes, planes) * 4 + xh * 2 + core

    def head_at(yy):
        return xl * ys + lax.rem(yy + ys, ys)

    partner = (z * 4 + xh * 2 + (1 - core), hi)
    across = (z * 4 + (1 - xh) * 2 + core, (1 - xl) * ys + y)
    beside = (ci, (1 - xl) * ys + y)
    z_next, z_prev = (ctx_at(z + 1), hi), (ctx_at(z - 1), hi)
    y_next, y_prev = (ci, head_at(y + 1)), (ci, head_at(y - 1))
    toward_z = (z_next, z_prev)
    toward_y = (y_next, y_prev)

    loads = [pltpu.make_async_copy(latent.at[0], kv.at[ci, 0:BLOCK, :], load_sem.at[0])]
    for i in range(4):
        loads.append(
            pltpu.make_async_copy(
                key_rope.at[0, 16 * i : 16 * i + 16, :],
                kv.at[ci, BLOCK:ROWS, 128 * i : 128 * i + 128],
                load_sem.at[1 + i],
            )
        )
    for i, (src, dst) in enumerate(
        ((q_nope, qn_buf), (w_uk, wuk_buf), (q_rope, qr_buf), (w_uv, wuv_buf))
    ):
        loads.append(pltpu.make_async_copy(src, dst, load_sem.at[5 + i]))
    width = w_mine.shape[1]
    cut = out.shape[0]
    quarter = w_mine.shape[0] // 4
    my_columns = pl.ds(pl.multiple_of(xl * width, width), width)
    peer_columns = pl.ds(pl.multiple_of((1 - xl) * width, width), width)
    loads.append(pltpu.make_async_copy(w_out.at[:, my_columns], w_mine, load_sem.at[9]))
    for copy in loads:
        copy.start()

    barrier = pltpu.get_barrier_semaphore()
    for device in (partner, across, beside, z_next, z_prev, y_next, y_prev):
        pl.semaphore_signal(barrier, inc=1, device_id=device, device_id_type=MESH)
    pl.semaphore_wait(barrier, 7)

    def part(block, p):
        return kv.at[block, THIRD * p : THIRD * (p + 1), :]

    def send(block, p, send_sem, recv_sem, device):
        return pltpu.make_async_remote_copy(
            part(block, p), part(block, p), send_sem, recv_sem, device_id=device, device_id_type=MESH
        )

    def plane_of(d, hop):
        return lax.rem(z + planes - hop, planes) if d == 0 else lax.rem(z + hop, planes)

    def mine(plane):
        return plane * 4 + color * 2 + core

    def other(plane):
        return plane * 4 + (1 - color) * 2 + core

    def z_copy(d, hop, p):
        return send(mine(plane_of(d, hop - 1)), p, z_send.at[d, hop - 1, p], z_recv.at[d, hop - 1, p], toward_z[d])

    def y_copy(d, hop, p):
        return send(mine(plane_of(d, hop)), p, y_send.at[d, hop - 1, p], y_recv.at[d, hop - 1, p], toward_y[d])

    def y_arrival(d, hop, p):
        return send(other(plane_of(d, hop)), p, y_send.at[d, hop - 1, p], y_recv.at[d, hop - 1, p], toward_y[d])

    def zp_copy(d, hop, p):
        return send(mine(plane_of(d, hop)), p, zp_send.at[d, hop - 1, p], zp_recv.at[d, hop - 1, p], partner)

    def yp_copy(d, hop, p):
        return send(other(plane_of(d, hop)), p, yp_send.at[d, hop - 1, p], yp_recv.at[d, hop - 1, p], partner)

    def carried(d, hop, p):
        return hop < 4 or (p < 2 if d == 0 else p == 2)

    for copy in loads[:5]:
        copy.wait()
    across_block = z * 4 + (1 - xh) * 2 + core
    x_copies = [send(ci, p, x_send.at[p], x_recv.at[p], across) for p in range(PIECES)]
    for copy in x_copies:
        copy.start()
    own_copy = pltpu.make_async_remote_copy(
        kv.at[ci], kv.at[ci], own_send.at[0], own_recv.at[0], device_id=partner, device_id_type=MESH
    )
    own_copy.start()

    @pl.when(xh == color)
    def _():
        for p in range(PIECES):
            for d in range(2):
                z_copy(d, 1, p).start()

    def w_rows(which, of_core):
        return pl.ds(pl.multiple_of((2 * of_core + which) * quarter, quarter), quarter)

    w_copies = [
        pltpu.make_async_remote_copy(
            w_out.at[w_rows(which, core), peer_columns],
            w_peer.at[w_rows(which, core), :],
            w_send.at[which],
            w_recv.at[which],
            device_id=device,
            device_id_type=MESH,
        )
        for which, device in enumerate((beside, across))
    ]
    wp_copies = [
        pltpu.make_async_remote_copy(
            w_peer.at[w_rows(which, core), :],
            w_peer.at[w_rows(which, core), :],
            w_send.at[2 + which],
            w_recv.at[2 + which],
            device_id=partner,
            device_id_type=MESH,
        )
        for which in range(2)
    ]
    for copy in w_copies:
        copy.start()

    block_ids = lax.broadcasted_iota(jnp.int32, (planes * 4, BLOCK), 0)
    listed = block_ids < 0
    for j in range(chosen.shape[1]):
        listed = jnp.logical_or(listed, block_ids == chosen[0, j])
    bias[...] = jnp.where(listed, 0.0, MASKED)
    row_max[...] = jnp.full_like(row_max, MASKED)
    row_sum[...] = jnp.zeros_like(row_sum)
    acc[...] = jnp.zeros_like(acc)

    xp_copies = [send(across_block, p, xp_send.at[p], xp_recv.at[p], partner) for p in range(PIECES)]
    for p in range(PIECES):
        x_copies[p].wait_recv()
        xp_copies[p].start()

        @pl.when(xh != color)
        def _():
            for d in range(2):
                z_copy(d, 1, p).start()

    for copy in loads[5:8]:
        copy.wait()
    for h in range(heads):
        rows = slice(BLOCK * h, BLOCK * (h + 1))
        q_lat[rows, :] = jnp.dot(
            qn_buf[:, QK_NOPE * h : QK_NOPE * (h + 1)], wuk_buf[h], preferred_element_type=jnp.float32
        ).astype(jnp.bfloat16)
        q_rot[rows, :] = qr_buf[:, ROPE * h : ROPE * (h + 1)]

    scale = (QK_NOPE + ROPE) ** -0.5 * math.log2(math.e)
    half = heads * BLOCK // 2

    def attend(plane, r, own):
        rows = slice(half * r, half * (r + 1))
        first = plane * 4
        keys = jnp.concatenate([kv[first + i, 0:BLOCK, :] for i in range(4)], axis=0)
        rotary = jnp.concatenate(
            [
                jnp.concatenate(
                    [kv[first + i, BLOCK:ROWS, 128 * j : 128 * (j + 1)] for j in range(4)], axis=0
                )
                for i in range(4)
            ],
            axis=1,
        )
        scores = lax.dot_general(
            q_lat[rows, :], keys, (((1,), (1,)), ((), ())), preferred_element_type=jnp.float32
        )
        scores = scores + jnp.dot(q_rot[rows, :], rotary, preferred_element_type=jnp.float32)
        hidden = jnp.concatenate([bias[pl.ds(first + i, 1), :] for i in range(4)], axis=1)
        scores = scores * scale + hidden
        if own:
            t_ids = lax.broadcasted_iota(jnp.int32, scores.shape, 0) % BLOCK
            col_ids = lax.broadcasted_iota(jnp.int32, scores.shape, 1)
            u_ids = col_ids - (ci % 4) * BLOCK
            later = (u_ids > t_ids) & (u_ids < BLOCK)
            scores = jnp.where(later, MASKED, scores)
        old_max = row_max[rows, :]
        new_max = jnp.maximum(old_max, jnp.max(scores, axis=1, keepdims=True))
        factor = jnp.exp2(old_max - new_max)
        wide = jnp.concatenate([new_max] * 4, axis=1)
        exponent = jnp.exp2(scores - wide)
        total = exponent[:, 0:128] + exponent[:, 128:256] + exponent[:, 256:384] + exponent[:, 384:512]
        row_max[rows, :] = new_max
        row_sum[rows, :] = row_sum[rows, :] * factor + total
        acc[rows, :] = acc[rows, :] * jnp.concatenate([factor] * 4, axis=1) + jnp.dot(
            exponent.astype(jnp.bfloat16), keys, preferred_element_type=jnp.float32
        )

    def turn(source, which):
        for j in range(width // 128):
            columns = slice(128 * j, 128 * (j + 1))
            w_turned[which, columns, :] = source[:, columns].T

    own_copy.wait_recv()
    for p in range(PIECES):
        xp_copies[p].wait_recv()

    def step(hop, c):
        for p in range(PIECES):
            for d in range(2):

                @pl.when((hop < 4) | ((hop == 4) & (p < 2 if d == 0 else p == 2)))
                def _():
                    z_copy(d, hop, p).wait_recv()

                @pl.when((hop < 3) | ((hop == 3) & (p < 2 if d == 0 else p == 2)))
                def _():
                    z_copy(d, hop + 1, p).start()

                @pl.when((hop < 4) | ((hop == 4) & (p < 2 if d == 0 else p == 2)))
                def _():
                    y_copy(d, hop, p).start()
                    zp_copy(d, hop, p).start()

            before = hop - 1
            for d in range(2):

                @pl.when((before >= 1) & ((before < 4) | ((before == 4) & (p < 2 if d == 0 else p == 2))))
                def _():
                    y_arrival(d, before, p).wait_recv()
                    yp_copy(d, before, p).start()

            if p == 0:

                @pl.when(hop == 1)
                def _():
                    for r in range(2):
                        attend(z, r, True)

            if p == 2:

                @pl.when(hop == 1)
                def _():
                    loads[9].wait()
                    turn(w_mine, 0)

                @pl.when(hop == 4)
                def _():
                    for copy in w_copies:
                        copy.wait_recv()
                    for copy in wp_copies:
                        copy.start()

                @pl.when(hop == 5)
                def _():
                    for copy in wp_copies:
                        copy.wait_recv()
                    turn(w_peer, 1)

            ready = hop - 2
            if p > 0:
                d = p - 1

                @pl.when((ready >= 1) & (ready < 4))
                def _():
                    for q in range(PIECES):
                        zp_copy(d, ready, q).wait_recv()
                        yp_copy(d, ready, q).wait_recv()
                    for r in range(2):
                        attend(plane_of(d, ready), r, False)

        return c

    lax.fori_loop(1, 6, step, 0)
    for d in range(2):
        for p in range(PIECES):
            if carried(d, 4, p):
                zp_copy(d, 4, p).wait_recv()
                yp_copy(d, 4, p).wait_recv()
    for r in range(2):
        attend(plane_of(0, 4), r, False)

    loads[8].wait()
    v_copies = []
    for h in range(heads):
        rows = slice(BLOCK * h, BLOCK * (h + 1))
        columns = slice(VHEAD * h, VHEAD * (h + 1))
        denominator = jnp.sum(row_sum[rows, :], axis=1, keepdims=True)
        mix = (acc[rows, :] / denominator).astype(jnp.bfloat16)
        values[:, columns] = jnp.dot(mix, wuv_buf[h], preferred_element_type=jnp.float32).astype(jnp.bfloat16)
        v_copies.append(
            pltpu.make_async_remote_copy(
                values.at[:, columns],
                v_peer.at[:, columns],
                v_send.at[h],
                v_recv.at[h],
                device_id=beside,
                device_id_type=MESH,
            )
        )
        v_copies[h].start()

    def owner(step):
        return lax.rem(y + step + 2 * ys, ys)

    def product(step, which, features):
        rows = pl.ds(pl.multiple_of(owner(step) * cut, 16), cut)
        return lax.dot_general(
            w_turned[which, rows, :],
            features[...],
            (((1,), (1,)), ((), ())),
            preferred_element_type=jnp.float32,
        )

    def own_part(step):
        piece[owner(step)] = product(step, 0, values)

    def peer_part(step):
        piece[owner(step)] += product(step, 1, v_peer)

    steps = [4, 3, -3, 2, -2, 1, -1, 0]
    for step_at in steps:
        own_part(step_at)
    for copy in v_copies:
        copy.wait_recv()

    rows_half = piece.shape[1] // 2

    def hops_of(d, t):
        return 4 if (d == 0) == (t == 0) else 3

    def r_copy(d, t, k):
        return pltpu.make_async_remote_copy(
            staged.at[d, t, k - 1],
            landed.at[d, t, k - 1],
            r_send.at[d, t, k - 1],
            r_recv.at[d, t, k - 1],
            device_id=toward_y[d],
            device_id_type=MESH,
        )

    def my_rows(step, t):
        return piece[owner(step), rows_half * t : rows_half * (t + 1), :]

    def send_sum(d, t, k):
        away = hops_of(d, t) - k + 1
        total = my_rows(away if d == 0 else -away, t)
        if k > 1:
            r_copy(d, t, k - 1).wait_recv()
            total = total + landed[d, t, k - 2].astype(jnp.float32)
        staged[d, t, k - 1] = total.astype(jnp.bfloat16)
        r_copy(d, t, k).start()

    chains = [(0, 0), (1, 1), (0, 1), (1, 0)]
    peer_part(4)
    send_sum(0, 0, 1)
    send_sum(1, 1, 1)
    peer_part(3)
    send_sum(0, 1, 1)
    peer_part(-3)
    send_sum(1, 0, 1)
    for step_at in (2, -2, 1, -1, 0):
        peer_part(step_at)
    for k in range(2, 5):
        for d, t in chains:
            if k <= hops_of(d, t):
                send_sum(d, t, k)
    for t in (1, 0):
        total = my_rows(0, t)
        for d in range(2):
            n = hops_of(d, t)
            r_copy(d, t, n).wait_recv()
            total = total + landed[d, t, n - 1].astype(jnp.float32)
        out[rows_half * t : rows_half * (t + 1), :] = total.astype(jnp.bfloat16)

    for d, t in chains:
        for k in range(1, hops_of(d, t) + 1):
            r_copy(d, t, k).wait_send()
    for copy in w_copies + wp_copies + v_copies:
        copy.wait_send()
    for copy in x_copies + xp_copies + [own_copy]:
        copy.wait_send()
    for d in range(2):
        for hop in range(1, 5):
            for p in range(PIECES):
                if carried(d, hop, p):
                    z_copy(d, hop, p).wait_send()
                    y_copy(d, hop, p).wait_send()
                    zp_copy(d, hop, p).wait_send()
                    yp_copy(d, hop, p).wait_send()


def solution(mesh):
    planes = mesh.shape["ctx"] // 4
    ys = mesh.shape["head"] // 2

    def on_device(q_nope, q_rope, latent, key_rope, chosen, w_uk, w_uv, w_out):
        heads = w_uk.shape[0]
        tokens = q_nope.shape[0]
        rows = heads * tokens
        anywhere = pl.BlockSpec(memory_space=pl.ANY)
        dma = pltpu.SemaphoreType.DMA

        def kernel(*refs):
            gather_attend(heads, planes, ys, *refs)

        depth = heads * VHEAD
        width = w_out.shape[1] // 2
        cut = width // ys
        return pl.pallas_call(
            kernel,
            out_shape=jax.ShapeDtypeStruct((cut, tokens), jnp.bfloat16),
            in_specs=[
                anywhere,
                anywhere,
                anywhere,
                anywhere,
                pl.BlockSpec(memory_space=pltpu.SMEM),
                anywhere,
                anywhere,
                anywhere,
            ],
            out_specs=pl.BlockSpec(memory_space=pltpu.VMEM),
            scratch_shapes=[
                pltpu.VMEM((planes * 4, ROWS, LAT), jnp.bfloat16),
                pltpu.VMEM(q_nope.shape, jnp.bfloat16),
                pltpu.VMEM(q_rope.shape, jnp.bfloat16),
                pltpu.VMEM(w_uk.shape, jnp.bfloat16),
                pltpu.VMEM(w_uv.shape, jnp.bfloat16),
                pltpu.VMEM((rows, LAT), jnp.bfloat16),
                pltpu.VMEM((rows, ROPE), jnp.bfloat16),
                pltpu.VMEM((planes * 4, BLOCK), jnp.float32),
                pltpu.VMEM((rows, 128), jnp.float32),
                pltpu.VMEM((rows, 128), jnp.float32),
                pltpu.VMEM((rows, LAT), jnp.float32),
                dma((10,)),
                dma((3,)),
                dma((3,)),
                dma((1,)),
                dma((1,)),
                dma((3,)),
                dma((3,)),
            ]
            + [dma((2, 4, 3))] * 8
            + [
                pltpu.VMEM((depth, width), jnp.bfloat16),
                pltpu.VMEM((depth, width), jnp.bfloat16),
                pltpu.VMEM((2, width, depth), jnp.bfloat16),
                pltpu.VMEM((tokens, depth), jnp.bfloat16),
                pltpu.VMEM((tokens, depth), jnp.bfloat16),
                pltpu.VMEM((ys, cut, tokens), jnp.float32),
                pltpu.VMEM((2, 2, 4, cut // 2, tokens), jnp.bfloat16),
                pltpu.VMEM((2, 2, 4, cut // 2, tokens), jnp.bfloat16),
                dma((4,)),
                dma((4,)),
                dma((heads,)),
                dma((heads,)),
                dma((2, 2, 4)),
                dma((2, 2, 4)),
            ],
            compiler_params=pltpu.CompilerParams(
                collective_id=0, has_side_effects=True, vmem_limit_bytes=67043328
            ),
        )(q_nope, q_rope, latent, key_rope, chosen, w_uk, w_uv, w_out).T

    return jax.shard_map(
        on_device,
        mesh=mesh,
        in_specs=(
            P("ctx", "head"),
            P("ctx", "head"),
            P("ctx", None, None),
            P("ctx", None, None),
            P("ctx", None),
            P("head", None, None),
            P("head", None, None),
            P("head", None),
        ),
        out_specs=P("ctx", "head"),
        check_vma=False,
    )
```

```python
import math

import jax
import jax.numpy as jnp
from jax import lax
from jax.experimental import pallas as pl
from jax.experimental.pallas import tpu as pltpu
from jax.sharding import PartitionSpec as P

LAT = 512
ROPE = 64
QK_NOPE = 128
VHEAD = 128
BLOCK = 128
ROWS = 144
THIRD = 48
PIECES = 3
MASKED = -1e30
MESH = pl.DeviceIdType.MESH


def gather_attend(
    heads,
    planes,
    ys,
    q_nope,
    q_rope,
    latent,
    key_rope,
    chosen_hbm,
    w_uk,
    w_uv,
    w_out,
    out,
    kv,
    qn_buf,
    qr_buf,
    wuk_buf,
    wuv_buf,
    q_lat,
    q_rot,
    bias,
    row_max,
    row_sum,
    acc,
    load_sem,
    x_send,
    x_recv,
    own_send,
    own_recv,
    xp_send,
    xp_recv,
    z_send,
    z_recv,
    y_send,
    y_recv,
    zp_send,
    zp_recv,
    yp_send,
    yp_recv,
    w_mine,
    w_peer,
    w_turned,
    values,
    v_peer,
    piece,
    staged,
    landed,
    w_send,
    w_recv,
    v_send,
    v_recv,
    r_send,
    r_recv,
    chosen,
):
    ci = lax.axis_index("ctx")
    hi = lax.axis_index("head")
    z, xh, core = ci // 4, (ci // 2) % 2, ci % 2
    xl, y = hi // ys, hi % ys
    color = y % 2

    def ctx_at(zz):
        return lax.rem(zz + planes, planes) * 4 + xh * 2 + core

    def head_at(yy):
        return xl * ys + lax.rem(yy + ys, ys)

    partner = (z * 4 + xh * 2 + (1 - core), hi)
    across = (z * 4 + (1 - xh) * 2 + core, (1 - xl) * ys + y)
    beside = (ci, (1 - xl) * ys + y)
    z_next, z_prev = (ctx_at(z + 1), hi), (ctx_at(z - 1), hi)
    y_next, y_prev = (ci, head_at(y + 1)), (ci, head_at(y - 1))
    z_over, z_under = (ctx_at(z + 2), hi), (ctx_at(z - 2), hi)
    y_over, y_under = (ci, head_at(y + 2)), (ci, head_at(y - 2))
    toward_z = ((z_next, z_prev), (z_over, z_under))
    toward_y = ((y_next, y_prev), (y_over, y_under))

    loads = [pltpu.make_async_copy(latent.at[0], kv.at[ci, 0:BLOCK, :], load_sem.at[0])]
    for i in range(4):
        loads.append(
            pltpu.make_async_copy(
                key_rope.at[0, 16 * i : 16 * i + 16, :],
                kv.at[ci, BLOCK:ROWS, 128 * i : 128 * i + 128],
                load_sem.at[1 + i],
            )
        )
    for i, (src, dst) in enumerate(
        ((q_nope, qn_buf), (w_uk, wuk_buf), (q_rope, qr_buf), (w_uv, wuv_buf))
    ):
        loads.append(pltpu.make_async_copy(src, dst, load_sem.at[5 + i]))
    width = w_mine.shape[1]
    cut = out.shape[0]
    quarter = w_mine.shape[0] // 4
    my_columns = pl.ds(pl.multiple_of(xl * width, width), width)
    peer_columns = pl.ds(pl.multiple_of((1 - xl) * width, width), width)
    loads.append(pltpu.make_async_copy(w_out.at[:, my_columns], w_mine, load_sem.at[9]))
    loads.append(pltpu.make_async_copy(chosen_hbm, chosen, load_sem.at[10]))
    for copy in loads:
        copy.start()

    barrier = pltpu.get_barrier_semaphore()
    greeted = (partner, across, beside) + toward_z[0] + toward_z[1] + toward_y[0] + toward_y[1]
    for device in greeted:
        pl.semaphore_signal(barrier, inc=1, device_id=device, device_id_type=MESH)
    pl.semaphore_wait(barrier, len(greeted))

    def part(block, p):
        return kv.at[block, THIRD * p : THIRD * (p + 1), :]

    def send(block, p, send_sem, recv_sem, device):
        return pltpu.make_async_remote_copy(
            part(block, p), part(block, p), send_sem, recv_sem, device_id=device, device_id_type=MESH
        )

    def plane_of(d, hop):
        return lax.rem(z + planes - hop, planes) if d == 0 else lax.rem(z + hop, planes)

    def mine(plane):
        return plane * 4 + color * 2 + core

    def other(plane):
        return plane * 4 + (1 - color) * 2 + core

    def z_copy(d, hop, p):
        source, stride = ((0, 1), (0, 2), (2, 1), (2, 2))[hop - 1]
        return send(
            mine(plane_of(d, source)), p, z_send.at[d, hop - 1, p], z_recv.at[d, hop - 1, p], toward_z[stride - 1][d]
        )

    def y_copy(d, hop, p):
        return send(mine(plane_of(d, hop)), p, y_send.at[d, hop - 1, p], y_recv.at[d, hop - 1, p], toward_y[0][d])

    def y_arrival(d, hop, p):
        return send(other(plane_of(d, hop)), p, y_send.at[d, hop - 1, p], y_recv.at[d, hop - 1, p], toward_y[0][d])

    def zp_copy(d, hop, p):
        return send(mine(plane_of(d, hop)), p, zp_send.at[d, hop - 1, p], zp_recv.at[d, hop - 1, p], partner)

    def yp_copy(d, hop, p):
        return send(other(plane_of(d, hop)), p, yp_send.at[d, hop - 1, p], yp_recv.at[d, hop - 1, p], partner)

    def carried(d, hop, p):
        return hop < 4 or (p < 2 if d == 0 else p == 2)

    for copy in loads[:5]:
        copy.wait()
    across_block = z * 4 + (1 - xh) * 2 + core
    x_copies = [send(ci, p, x_send.at[p], x_recv.at[p], across) for p in range(PIECES)]
    for copy in x_copies:
        copy.start()
    own_copy = pltpu.make_async_remote_copy(
        kv.at[ci], kv.at[ci], own_send.at[0], own_recv.at[0], device_id=partner, device_id_type=MESH
    )
    own_copy.start()

    @pl.when(xh == color)
    def _():
        for hop in (2, 1):
            for p in range(PIECES):
                for d in range(2):
                    z_copy(d, hop, p).start()

    def w_rows(which, of_core):
        return pl.ds(pl.multiple_of((2 * of_core + which) * quarter, quarter), quarter)

    w_copies = [
        pltpu.make_async_remote_copy(
            w_out.at[w_rows(which, core), peer_columns],
            w_peer.at[w_rows(which, core), :],
            w_send.at[which],
            w_recv.at[which],
            device_id=device,
            device_id_type=MESH,
        )
        for which, device in enumerate((beside, across))
    ]
    wp_copies = [
        pltpu.make_async_remote_copy(
            w_peer.at[w_rows(which, core), :],
            w_peer.at[w_rows(which, core), :],
            w_send.at[2 + which],
            w_recv.at[2 + which],
            device_id=partner,
            device_id_type=MESH,
        )
        for which in range(2)
    ]
    for copy in w_copies:
        copy.start()

    loads[10].wait()
    block_ids = lax.broadcasted_iota(jnp.int32, (planes * 4, BLOCK), 0)
    listed = block_ids < 0
    for j in range(chosen.shape[1]):
        listed = jnp.logical_or(listed, block_ids == chosen[0, j])
    bias[...] = jnp.where(listed, 0.0, MASKED)
    row_max[...] = jnp.full_like(row_max, MASKED)
    row_sum[...] = jnp.zeros_like(row_sum)
    acc[...] = jnp.zeros_like(acc)

    xp_copies = [send(across_block, p, xp_send.at[p], xp_recv.at[p], partner) for p in range(PIECES)]
    for p in range(PIECES):
        x_copies[p].wait_recv()
        xp_copies[p].start()

        @pl.when(xh != color)
        def _():
            for d in range(2):
                z_copy(d, 2, p).start()

    @pl.when(xh != color)
    def _():
        for p in range(PIECES):
            for d in range(2):
                z_copy(d, 1, p).start()

    for copy in loads[5:8]:
        copy.wait()
    for h in range(heads):
        rows = slice(BLOCK * h, BLOCK * (h + 1))
        q_lat[rows, :] = jnp.dot(
            qn_buf[:, QK_NOPE * h : QK_NOPE * (h + 1)], wuk_buf[h], preferred_element_type=jnp.float32
        ).astype(jnp.bfloat16)
        q_rot[rows, :] = qr_buf[:, ROPE * h : ROPE * (h + 1)]

    scale = (QK_NOPE + ROPE) ** -0.5 * math.log2(math.e)
    half = heads * BLOCK // 2

    def attend(plane, r, own=False):
        rows = pl.ds(r * half, half)
        first = plane * 4
        keys = jnp.concatenate([kv[first + i, 0:BLOCK, :] for i in range(4)], axis=0)
        rotary = jnp.concatenate(
            [
                jnp.concatenate(
                    [kv[first + i, BLOCK:ROWS, 128 * j : 128 * (j + 1)] for j in range(4)], axis=0
                )
                for i in range(4)
            ],
            axis=1,
        )
        scores = lax.dot_general(
            q_lat[rows, :], keys, (((1,), (1,)), ((), ())), preferred_element_type=jnp.float32
        )
        scores = scores + jnp.dot(q_rot[rows, :], rotary, preferred_element_type=jnp.float32)
        hidden = jnp.concatenate([bias[pl.ds(first + i, 1), :] for i in range(4)], axis=1)
        scores = scores * scale + hidden
        if own:
            t_ids = lax.broadcasted_iota(jnp.int32, scores.shape, 0) % BLOCK
            col_ids = lax.broadcasted_iota(jnp.int32, scores.shape, 1)
            u_ids = col_ids - (ci % 4) * BLOCK
            later = (u_ids > t_ids) & (u_ids < BLOCK)
            scores = jnp.where(later, MASKED, scores)
        old_max = row_max[rows, :]
        new_max = jnp.maximum(old_max, jnp.max(scores, axis=1, keepdims=True))
        factor = jnp.exp2(old_max - new_max)
        wide = jnp.concatenate([new_max] * 4, axis=1)
        exponent = jnp.exp2(scores - wide)
        total = exponent[:, 0:128] + exponent[:, 128:256] + exponent[:, 256:384] + exponent[:, 384:512]
        row_max[rows, :] = new_max
        row_sum[rows, :] = row_sum[rows, :] * factor + total
        acc[rows, :] = acc[rows, :] * jnp.concatenate([factor] * 4, axis=1) + jnp.dot(
            exponent.astype(jnp.bfloat16), keys, preferred_element_type=jnp.float32
        )

    def turn(source, which):
        for j in range(width // 128):
            columns = slice(128 * j, 128 * (j + 1))
            w_turned[which, columns, :] = source[:, columns].T

    def attend_plane(plane, own=False):
        def turn_of(r, c):
            attend(plane, pl.multiple_of(r, 1), own)
            return c

        lax.fori_loop(0, 2, turn_of, 0)

    def z_take(d, hop, p):
        if carried(d, hop, p):
            z_copy(d, hop, p).wait_recv()
            if hop == 2:
                z_copy(d, 3, p).start()
                if carried(d, 4, p):
                    z_copy(d, 4, p).start()
            y_copy(d, hop, p).start()
            zp_copy(d, hop, p).start()

    def y_take(d, hop, p):
        if carried(d, hop, p):
            y_arrival(d, hop, p).wait_recv()
            yp_copy(d, hop, p).start()

    def complete(d, hop):
        for p in range(PIECES):
            if carried(d, hop, p):
                zp_copy(d, hop, p).wait_recv()
                yp_copy(d, hop, p).wait_recv()

    def visit(d, hop):
        complete(d, hop)
        attend_plane(plane_of(d, hop))

    both = range(2)
    for d in both:
        z_take(d, 2, 0)
    own_copy.wait_recv()
    for p in range(PIECES):
        xp_copies[p].wait_recv()
    attend_plane(z, True)
    for p in (1, 2):
        for d in both:
            z_take(d, 2, p)
    loads[9].wait()
    turn(w_mine, 0)
    for p in range(PIECES):
        for d in both:
            z_take(d, 1, p)
        for d in both:
            y_take(d, 2, p)
    for copy in w_copies:
        copy.wait_recv()
    for copy in wp_copies:
        copy.start()
    for p in range(PIECES):
        for d in both:
            z_take(d, 3, p)
        for d in both:
            z_take(d, 4, p)
        for d in both:
            y_take(d, 1, p)
        if p == 0:
            visit(0, 2)
        if p == 1:
            visit(1, 2)
    visit(0, 1)
    for p in range(PIECES):
        for d in both:
            y_take(d, 3, p)
        for d in both:
            y_take(d, 4, p)
        if p == 0:
            visit(1, 1)
        if p == 1:
            for copy in wp_copies:
                copy.wait_recv()
            turn(w_peer, 1)
    visit(0, 3)
    visit(1, 3)
    for d in both:
        complete(d, 4)

    loads[8].wait()
    v_copies = []
    for r in range(2):
        attend(plane_of(0, 4), r)
        for h in range(heads // 2 * r, heads // 2 * (r + 1)):
            rows = slice(BLOCK * h, BLOCK * (h + 1))
            columns = slice(VHEAD * h, VHEAD * (h + 1))
            denominator = jnp.sum(row_sum[rows, :], axis=1, keepdims=True)
            mix = (acc[rows, :] / denominator).astype(jnp.bfloat16)
            values[:, columns] = jnp.dot(mix, wuv_buf[h], preferred_element_type=jnp.float32).astype(jnp.bfloat16)
            v_copies.append(
                pltpu.make_async_remote_copy(
                    values.at[:, columns],
                    v_peer.at[:, columns],
                    v_send.at[h],
                    v_recv.at[h],
                    device_id=beside,
                    device_id_type=MESH,
                )
            )
            v_copies[h].start()

    def owner(step):
        return lax.rem(y + step + 2 * ys, ys)

    def product(step, which, features):
        rows = pl.ds(pl.multiple_of(owner(step) * cut, 16), cut)
        return lax.dot_general(
            w_turned[which, rows, :],
            features[...],
            (((1,), (1,)), ((), ())),
            preferred_element_type=jnp.float32,
        )

    def own_part(step):
        piece[owner(step)] = product(step, 0, values)

    def peer_part(step):
        piece[owner(step)] += product(step, 1, v_peer)

    steps = [4, 3, -3, 1, -1, 2, -2, 0]
    for away in steps:
        own_part(away)
    for copy in v_copies:
        copy.wait_recv()

    rows_half = piece.shape[1] // 2
    sign = (1, -1)

    def r_copy(d, away, t):
        slot = {4: 0, 3: 1 + t, 1: 3 + t, 2: 5 + t}[away]
        stride = {4: 2, 3: 1, 1: 1, 2: 2}[away]
        return pltpu.make_async_remote_copy(
            staged.at[d, slot],
            landed.at[d, slot],
            r_send.at[d, slot],
            r_recv.at[d, slot],
            device_id=toward_y[stride - 1][d],
            device_id_type=MESH,
        )

    def take_sum(d, away, t):
        r_copy(d, away, t).wait_recv()
        return landed[d, {4: 0, 3: 1 + t, 1: 3 + t, 2: 5 + t}[away]].astype(jnp.float32)

    def send_sum(d, away, t):
        total = piece[owner(sign[d] * away), rows_half * t : rows_half * (t + 1), :]
        if away == 2:
            total = total + take_sum(d, 3, t)
            if t == d:
                total = total + take_sum(d, 4, t)
        staged[d, {4: 0, 3: 1 + t, 1: 3 + t, 2: 5 + t}[away]] = total.astype(jnp.bfloat16)
        r_copy(d, away, t).start()

    peer_part(4)
    for d in both:
        send_sum(d, 4, d)
    for away in (3, 1):
        for d in both:
            peer_part(sign[d] * away)
            for t in (d, 1 - d):
                send_sum(d, away, t)
    for away in (2, -2, 0):
        peer_part(away)
    for i in range(2):
        for d in both:
            send_sum(d, 2, (1 - d, d)[i])
    mine_of = [piece[owner(0), rows_half * t : rows_half * (t + 1), :] for t in range(2)]
    for t in range(2):
        for d in both:
            mine_of[t] = mine_of[t] + take_sum(d, 1, t)
    for t in range(2):
        for d in both:
            mine_of[t] = mine_of[t] + take_sum(d, 2, t)
        out[rows_half * t : rows_half * (t + 1), :] = mine_of[t].astype(jnp.bfloat16)

    for d in both:
        r_copy(d, 4, d).wait_send()
        for away in (3, 1, 2):
            for t in range(2):
                r_copy(d, away, t).wait_send()
    for copy in w_copies + wp_copies + v_copies:
        copy.wait_send()
    for copy in x_copies + xp_copies + [own_copy]:
        copy.wait_send()
    for d in range(2):
        for hop in range(1, 5):
            for p in range(PIECES):
                if carried(d, hop, p):
                    z_copy(d, hop, p).wait_send()
                    y_copy(d, hop, p).wait_send()
                    zp_copy(d, hop, p).wait_send()
                    yp_copy(d, hop, p).wait_send()


def solution(mesh):
    planes = mesh.shape["ctx"] // 4
    ys = mesh.shape["head"] // 2

    def on_device(q_nope, q_rope, latent, key_rope, chosen, w_uk, w_uv, w_out):
        heads = w_uk.shape[0]
        tokens = q_nope.shape[0]
        rows = heads * tokens
        anywhere = pl.BlockSpec(memory_space=pl.ANY)
        dma = pltpu.SemaphoreType.DMA

        def kernel(*refs):
            gather_attend(heads, planes, ys, *refs)

        depth = heads * VHEAD
        width = w_out.shape[1] // 2
        cut = width // ys
        return pl.pallas_call(
            kernel,
            out_shape=jax.ShapeDtypeStruct((cut, tokens), jnp.bfloat16),
            in_specs=[anywhere] * 8,
            out_specs=pl.BlockSpec(memory_space=pltpu.VMEM),
            scratch_shapes=[
                pltpu.VMEM((planes * 4, ROWS, LAT), jnp.bfloat16),
                pltpu.VMEM(q_nope.shape, jnp.bfloat16),
                pltpu.VMEM(q_rope.shape, jnp.bfloat16),
                pltpu.VMEM(w_uk.shape, jnp.bfloat16),
                pltpu.VMEM(w_uv.shape, jnp.bfloat16),
                pltpu.VMEM((rows, LAT), jnp.bfloat16),
                pltpu.VMEM((rows, ROPE), jnp.bfloat16),
                pltpu.VMEM((planes * 4, BLOCK), jnp.float32),
                pltpu.VMEM((rows, 128), jnp.float32),
                pltpu.VMEM((rows, 128), jnp.float32),
                pltpu.VMEM((rows, LAT), jnp.float32),
                dma((11,)),
                dma((3,)),
                dma((3,)),
                dma((1,)),
                dma((1,)),
                dma((3,)),
                dma((3,)),
            ]
            + [dma((2, 4, 3))] * 8
            + [
                pltpu.VMEM((depth, width), jnp.bfloat16),
                pltpu.VMEM((depth, width), jnp.bfloat16),
                pltpu.VMEM((2, width, depth), jnp.bfloat16),
                pltpu.VMEM((tokens, depth), jnp.bfloat16),
                pltpu.VMEM((tokens, depth), jnp.bfloat16),
                pltpu.VMEM((ys, cut, tokens), jnp.float32),
                pltpu.VMEM((2, 7, cut // 2, tokens), jnp.bfloat16),
                pltpu.VMEM((2, 7, cut // 2, tokens), jnp.bfloat16),
                dma((4,)),
                dma((4,)),
                dma((heads,)),
                dma((heads,)),
                dma((2, 7)),
                dma((2, 7)),
                pltpu.SMEM(chosen.shape, jnp.int32),
            ],
            compiler_params=pltpu.CompilerParams(
                collective_id=0, has_side_effects=True, vmem_limit_bytes=67043328
            ),
        )(q_nope, q_rope, latent, key_rope, chosen, w_uk, w_uv, w_out).T

    return jax.shard_map(
        on_device,
        mesh=mesh,
        in_specs=(
            P("ctx", "head"),
            P("ctx", "head"),
            P("ctx", None, None),
            P("ctx", None, None),
            P("ctx", None),
            P("head", None, None),
            P("head", None, None),
            P("head", None),
        ),
        out_specs=P("ctx", "head"),
        check_vma=False,
    )
```

```python
import math

import jax
import jax.numpy as jnp
from jax import lax
from jax.experimental import pallas as pl
from jax.experimental.pallas import tpu as pltpu
from jax.sharding import PartitionSpec as P

LAT = 512
ROPE = 64
QK_NOPE = 128
VHEAD = 128
BLOCK = 128
ROWS = 144
THIRD = 48
PIECES = 3
MASKED = -1e30
MESH = pl.DeviceIdType.MESH


def gather_attend(
    heads,
    planes,
    ys,
    q_nope,
    q_rope,
    latent,
    key_rope,
    chosen_hbm,
    w_uk,
    w_uv,
    w_out,
    out,
    kv,
    qn_buf,
    qr_buf,
    wuk_buf,
    wuv_buf,
    q_lat,
    q_rot,
    bias,
    row_max,
    row_sum,
    acc,
    load_sem,
    x_send,
    x_recv,
    own_send,
    own_recv,
    xp_send,
    xp_recv,
    z_send,
    z_recv,
    y_send,
    y_recv,
    zp_send,
    zp_recv,
    yp_send,
    yp_recv,
    w_mine,
    w_peer,
    w_turned,
    values,
    v_peer,
    piece,
    staged,
    landed,
    w_send,
    w_recv,
    v_send,
    v_recv,
    r_send,
    r_recv,
    chosen,
):
    ci = lax.axis_index("ctx")
    hi = lax.axis_index("head")
    z, xh, core = ci // 4, (ci // 2) % 2, ci % 2
    xl, y = hi // ys, hi % ys
    color = y % 2

    def ctx_at(zz):
        return lax.rem(zz + planes, planes) * 4 + xh * 2 + core

    def head_at(yy):
        return xl * ys + lax.rem(yy + ys, ys)

    partner = (z * 4 + xh * 2 + (1 - core), hi)
    across = (z * 4 + (1 - xh) * 2 + core, (1 - xl) * ys + y)
    beside = (ci, (1 - xl) * ys + y)
    z_next, z_prev = (ctx_at(z + 1), hi), (ctx_at(z - 1), hi)
    y_next, y_prev = (ci, head_at(y + 1)), (ci, head_at(y - 1))
    z_over, z_under = (ctx_at(z + 2), hi), (ctx_at(z - 2), hi)
    y_over, y_under = (ci, head_at(y + 2)), (ci, head_at(y - 2))
    toward_z = ((z_next, z_prev), (z_over, z_under))
    toward_y = ((y_next, y_prev), (y_over, y_under))

    loads = [pltpu.make_async_copy(latent.at[0], kv.at[ci, 0:BLOCK, :], load_sem.at[0])]
    for i in range(4):
        loads.append(
            pltpu.make_async_copy(
                key_rope.at[0, 16 * i : 16 * i + 16, :],
                kv.at[ci, BLOCK:ROWS, 128 * i : 128 * i + 128],
                load_sem.at[1 + i],
            )
        )
    for i, (src, dst) in enumerate(
        ((q_nope, qn_buf), (w_uk, wuk_buf), (q_rope, qr_buf), (w_uv, wuv_buf))
    ):
        loads.append(pltpu.make_async_copy(src, dst, load_sem.at[5 + i]))
    width = w_mine.shape[1]
    cut = out.shape[0]
    quarter = w_mine.shape[0] // 4
    my_columns = pl.ds(pl.multiple_of(xl * width, width), width)
    peer_columns = pl.ds(pl.multiple_of((1 - xl) * width, width), width)
    loads.append(pltpu.make_async_copy(w_out.at[:, my_columns], w_mine, load_sem.at[9]))
    loads.append(pltpu.make_async_copy(chosen_hbm, chosen, load_sem.at[10]))
    for copy in loads:
        copy.start()

    barrier = pltpu.get_barrier_semaphore()
    greeted = (partner, across, beside) + toward_z[0] + toward_z[1] + toward_y[0] + toward_y[1]
    for device in greeted:
        pl.semaphore_signal(barrier, inc=1, device_id=device, device_id_type=MESH)
    pl.semaphore_wait(barrier, len(greeted))

    def part(block, p):
        return kv.at[block, THIRD * p : THIRD * (p + 1), :]

    def send(block, p, send_sem, recv_sem, device):
        return pltpu.make_async_remote_copy(
            part(block, p), part(block, p), send_sem, recv_sem, device_id=device, device_id_type=MESH
        )

    def plane_of(d, hop):
        return lax.rem(z + planes - hop, planes) if d == 0 else lax.rem(z + hop, planes)

    def mine(plane):
        return plane * 4 + color * 2 + core

    def other(plane):
        return plane * 4 + (1 - color) * 2 + core

    def z_copy(d, hop, p):
        source, stride = ((0, 1), (1, 1), (2, 1), (2, 2))[hop - 1]
        return send(
            mine(plane_of(d, source)), p, z_send.at[d, hop - 1, p], z_recv.at[d, hop - 1, p], toward_z[stride - 1][d]
        )

    def y_copy(d, hop, p):
        return send(mine(plane_of(d, hop)), p, y_send.at[d, hop - 1, p], y_recv.at[d, hop - 1, p], toward_y[0][d])

    def y_arrival(d, hop, p):
        return send(other(plane_of(d, hop)), p, y_send.at[d, hop - 1, p], y_recv.at[d, hop - 1, p], toward_y[0][d])

    def zp_copy(d, hop, p):
        return send(mine(plane_of(d, hop)), p, zp_send.at[d, hop - 1, p], zp_recv.at[d, hop - 1, p], partner)

    def yp_copy(d, hop, p):
        return send(other(plane_of(d, hop)), p, yp_send.at[d, hop - 1, p], yp_recv.at[d, hop - 1, p], partner)

    def carried(d, hop, p):
        return hop < 4 or (p < 2 if d == 0 else p == 2)

    for copy in loads[:5]:
        copy.wait()
    across_block = z * 4 + (1 - xh) * 2 + core
    x_copies = [send(ci, p, x_send.at[p], x_recv.at[p], across) for p in range(PIECES)]
    for copy in x_copies:
        copy.start()
    own_copy = pltpu.make_async_remote_copy(
        kv.at[ci], kv.at[ci], own_send.at[0], own_recv.at[0], device_id=partner, device_id_type=MESH
    )
    own_copy.start()

    @pl.when(xh == color)
    def _():
        for p in range(PIECES):
            for d in range(2):
                z_copy(d, 1, p).start()

    def w_rows(which, of_core):
        return pl.ds(pl.multiple_of((2 * of_core + which) * quarter, quarter), quarter)

    w_copies = [
        pltpu.make_async_remote_copy(
            w_out.at[w_rows(which, core), peer_columns],
            w_peer.at[w_rows(which, core), :],
            w_send.at[which],
            w_recv.at[which],
            device_id=device,
            device_id_type=MESH,
        )
        for which, device in enumerate((beside, across))
    ]
    wp_copies = [
        pltpu.make_async_remote_copy(
            w_peer.at[w_rows(which, core), :],
            w_peer.at[w_rows(which, core), :],
            w_send.at[2 + which],
            w_recv.at[2 + which],
            device_id=partner,
            device_id_type=MESH,
        )
        for which in range(2)
    ]
    for copy in w_copies:
        copy.start()

    loads[10].wait()
    block_ids = lax.broadcasted_iota(jnp.int32, (planes * 4, BLOCK), 0)
    listed = block_ids < 0
    for j in range(chosen.shape[1]):
        listed = jnp.logical_or(listed, block_ids == chosen[0, j])
    bias[...] = jnp.where(listed, 0.0, MASKED)
    row_max[...] = jnp.full_like(row_max, MASKED)
    row_sum[...] = jnp.zeros_like(row_sum)
    acc[...] = jnp.zeros_like(acc)

    xp_copies = [send(across_block, p, xp_send.at[p], xp_recv.at[p], partner) for p in range(PIECES)]
    for p in range(PIECES):
        x_copies[p].wait_recv()
        xp_copies[p].start()

        @pl.when(xh != color)
        def _():
            for d in range(2):
                z_copy(d, 1, p).start()

    for copy in loads[5:8]:
        copy.wait()
    for h in range(heads):
        rows = slice(BLOCK * h, BLOCK * (h + 1))
        q_lat[rows, :] = jnp.dot(
            qn_buf[:, QK_NOPE * h : QK_NOPE * (h + 1)], wuk_buf[h], preferred_element_type=jnp.float32
        ).astype(jnp.bfloat16)
        q_rot[rows, :] = qr_buf[:, ROPE * h : ROPE * (h + 1)]

    scale = (QK_NOPE + ROPE) ** -0.5 * math.log2(math.e)
    half = heads * BLOCK // 2

    def attend(blocks, r, own=False):
        rows = slice(r * half, (r + 1) * half)
        keys = jnp.concatenate([kv[b, 0:BLOCK, :] for b in blocks], axis=0)
        rotary = jnp.concatenate(
            [
                jnp.concatenate([kv[b, BLOCK:ROWS, 128 * j : 128 * (j + 1)] for j in range(4)], axis=0)
                for b in blocks
            ],
            axis=1,
        )
        scores = lax.dot_general(
            q_lat[rows, :], keys, (((1,), (1,)), ((), ())), preferred_element_type=jnp.float32
        )
        scores = scores + jnp.dot(q_rot[rows, :], rotary, preferred_element_type=jnp.float32)
        hidden = jnp.concatenate([bias[pl.ds(b, 1), :] for b in blocks], axis=1)
        scores = scores * scale + hidden
        if own:
            t_ids = lax.broadcasted_iota(jnp.int32, scores.shape, 0) % BLOCK
            col_ids = lax.broadcasted_iota(jnp.int32, scores.shape, 1)
            u_ids = col_ids - (ci % 4) * BLOCK
            later = (u_ids > t_ids) & (u_ids < BLOCK)
            scores = jnp.where(later, MASKED, scores)
        old_max = row_max[rows, :]
        new_max = jnp.maximum(old_max, jnp.max(scores, axis=1, keepdims=True))
        factor = jnp.exp2(old_max - new_max)
        wide = jnp.concatenate([new_max] * len(blocks), axis=1)
        exponent = jnp.exp2(scores - wide)
        total = sum(exponent[:, 128 * i : 128 * (i + 1)] for i in range(1, len(blocks))) + exponent[:, 0:128]
        row_max[rows, :] = new_max
        row_sum[rows, :] = row_sum[rows, :] * factor + total
        acc[rows, :] = acc[rows, :] * jnp.concatenate([factor] * 4, axis=1) + jnp.dot(
            exponent.astype(jnp.bfloat16), keys, preferred_element_type=jnp.float32
        )

    def turn(source, which):
        for j in range(width // 128):
            columns = slice(128 * j, 128 * (j + 1))
            w_turned[which, columns, :] = source[:, columns].T

    both = range(2)

    def z_take(hop, p):
        for d in both:
            if carried(d, hop, p):
                z_copy(d, hop, p).wait_recv()
                for later in {1: (2,), 2: (3, 4)}.get(hop, ()):
                    if carried(d, later, p):
                        z_copy(d, later, p).start()
        for d in both:
            if carried(d, hop, p):
                y_copy(d, hop, p).start()
                zp_copy(d, hop, p).start()

    def y_take(hop, p):
        for d in both:
            if carried(d, hop, p):
                y_arrival(d, hop, p).wait_recv()
                yp_copy(d, hop, p).start()

    def chunk(hop, by_z):
        for d in both:
            for p in range(PIECES):
                if carried(d, hop, p):
                    (zp_copy if by_z else yp_copy)(d, hop, p).wait_recv()
        which = color if by_z else 1 - color
        firsts = [plane_of(d, hop) * 4 + which * 2 for d in both[: 1 if hop == 4 else 2]]
        return [first + i for first in firsts for i in range(2)]

    z_take(1, 0)
    own_copy.wait_recv()
    for p in range(PIECES):
        xp_copies[p].wait_recv()
    own_plane = [z * 4 + i for i in range(4)]
    attend(own_plane, 0, True)
    z_take(1, 1)
    attend(own_plane, 1, True)
    z_take(1, 2)
    blocks = chunk(1, True)
    attend(blocks, 0)
    z_take(2, 0)
    y_take(1, 0)
    attend(blocks, 1)
    z_take(2, 1)
    y_take(1, 1)
    loads[9].wait()
    turn(w_mine, 0)
    z_take(2, 2)
    y_take(1, 2)
    blocks = chunk(2, True)
    attend(blocks, 0)
    z_take(3, 0)
    y_take(2, 0)
    attend(blocks, 1)
    for copy in w_copies:
        copy.wait_recv()
    for copy in wp_copies:
        copy.start()
    z_take(3, 1)
    y_take(2, 1)
    blocks = chunk(1, False)
    attend(blocks, 0)
    z_take(3, 2)
    y_take(2, 2)
    attend(blocks, 1)
    for p in range(PIECES):
        z_take(4, p)
    for copy in wp_copies:
        copy.wait_recv()
    turn(w_peer, 1)
    blocks = chunk(2, False)
    attend(blocks, 0)
    y_take(3, 0)
    attend(blocks, 1)
    y_take(3, 1)
    blocks = chunk(3, True)
    attend(blocks, 0)
    y_take(3, 2)
    attend(blocks, 1)
    for p in range(PIECES):
        y_take(4, p)
    blocks = chunk(4, True)
    attend(blocks, 0)
    attend(blocks, 1)
    blocks = chunk(3, False)
    attend(blocks, 0)
    attend(blocks, 1)
    blocks = chunk(4, False)

    loads[8].wait()
    v_copies = []
    for r in range(2):
        attend(blocks, r)
        for h in range(heads // 2 * r, heads // 2 * (r + 1)):
            rows = slice(BLOCK * h, BLOCK * (h + 1))
            columns = slice(VHEAD * h, VHEAD * (h + 1))
            denominator = jnp.sum(row_sum[rows, :], axis=1, keepdims=True)
            mix = (acc[rows, :] / denominator).astype(jnp.bfloat16)
            values[:, columns] = jnp.dot(mix, wuv_buf[h], preferred_element_type=jnp.float32).astype(jnp.bfloat16)
            v_copies.append(
                pltpu.make_async_remote_copy(
                    values.at[:, columns],
                    v_peer.at[:, columns],
                    v_send.at[h],
                    v_recv.at[h],
                    device_id=beside,
                    device_id_type=MESH,
                )
            )
            v_copies[h].start()

    def owner(step):
        return lax.rem(y + step + 2 * ys, ys)

    def product(step, which, features):
        rows = pl.ds(pl.multiple_of(owner(step) * cut, 16), cut)
        return lax.dot_general(
            w_turned[which, rows, :],
            features[...],
            (((1,), (1,)), ((), ())),
            preferred_element_type=jnp.float32,
        )

    def own_part(step):
        piece[owner(step)] = product(step, 0, values)

    def peer_part(step):
        piece[owner(step)] += product(step, 1, v_peer)

    steps = [4, 3, -3, 1, -1, 2, -2, 0]
    for away in steps:
        own_part(away)
    for copy in v_copies:
        copy.wait_recv()

    rows_half = piece.shape[1] // 2
    sign = (1, -1)

    def r_copy(d, away, t):
        slot = {4: 0, 3: 1 + t, 1: 3 + t, 2: 5 + t}[away]
        stride = {4: 2, 3: 1, 1: 1, 2: 2}[away]
        return pltpu.make_async_remote_copy(
            staged.at[d, slot],
            landed.at[d, slot],
            r_send.at[d, slot],
            r_recv.at[d, slot],
            device_id=toward_y[stride - 1][d],
            device_id_type=MESH,
        )

    def take_sum(d, away, t):
        r_copy(d, away, t).wait_recv()
        return landed[d, {4: 0, 3: 1 + t, 1: 3 + t, 2: 5 + t}[away]].astype(jnp.float32)

    def send_sum(d, away, t):
        total = piece[owner(sign[d] * away), rows_half * t : rows_half * (t + 1), :]
        if away == 2:
            total = total + take_sum(d, 3, t)
            if t == d:
                total = total + take_sum(d, 4, t)
        staged[d, {4: 0, 3: 1 + t, 1: 3 + t, 2: 5 + t}[away]] = total.astype(jnp.bfloat16)
        r_copy(d, away, t).start()

    peer_part(4)
    for d in both:
        send_sum(d, 4, d)
    for away in (3, 1):
        for d in both:
            peer_part(sign[d] * away)
            for t in (d, 1 - d):
                send_sum(d, away, t)
    for away in (2, -2, 0):
        peer_part(away)
    for i in range(2):
        for d in both:
            send_sum(d, 2, (1 - d, d)[i])
    mine_of = [piece[owner(0), rows_half * t : rows_half * (t + 1), :] for t in range(2)]
    for t in range(2):
        for d in both:
            mine_of[t] = mine_of[t] + take_sum(d, 1, t)
    for t in range(2):
        for d in both:
            mine_of[t] = mine_of[t] + take_sum(d, 2, t)
        out[rows_half * t : rows_half * (t + 1), :] = mine_of[t].astype(jnp.bfloat16)

    for d in both:
        r_copy(d, 4, d).wait_send()
        for away in (3, 1, 2):
            for t in range(2):
                r_copy(d, away, t).wait_send()
    for copy in w_copies + wp_copies + v_copies:
        copy.wait_send()
    for copy in x_copies + xp_copies + [own_copy]:
        copy.wait_send()
    for d in range(2):
        for hop in range(1, 5):
            for p in range(PIECES):
                if carried(d, hop, p):
                    z_copy(d, hop, p).wait_send()
                    y_copy(d, hop, p).wait_send()
                    zp_copy(d, hop, p).wait_send()
                    yp_copy(d, hop, p).wait_send()


def solution(mesh):
    planes = mesh.shape["ctx"] // 4
    ys = mesh.shape["head"] // 2

    def on_device(q_nope, q_rope, latent, key_rope, chosen, w_uk, w_uv, w_out):
        heads = w_uk.shape[0]
        tokens = q_nope.shape[0]
        rows = heads * tokens
        anywhere = pl.BlockSpec(memory_space=pl.ANY)
        dma = pltpu.SemaphoreType.DMA

        def kernel(*refs):
            gather_attend(heads, planes, ys, *refs)

        depth = heads * VHEAD
        width = w_out.shape[1] // 2
        cut = width // ys
        return pl.pallas_call(
            kernel,
            out_shape=jax.ShapeDtypeStruct((cut, tokens), jnp.bfloat16),
            in_specs=[anywhere] * 8,
            out_specs=pl.BlockSpec(memory_space=pltpu.VMEM),
            scratch_shapes=[
                pltpu.VMEM((planes * 4, ROWS, LAT), jnp.bfloat16),
                pltpu.VMEM(q_nope.shape, jnp.bfloat16),
                pltpu.VMEM(q_rope.shape, jnp.bfloat16),
                pltpu.VMEM(w_uk.shape, jnp.bfloat16),
                pltpu.VMEM(w_uv.shape, jnp.bfloat16),
                pltpu.VMEM((rows, LAT), jnp.bfloat16),
                pltpu.VMEM((rows, ROPE), jnp.bfloat16),
                pltpu.VMEM((planes * 4, BLOCK), jnp.float32),
                pltpu.VMEM((rows, 128), jnp.float32),
                pltpu.VMEM((rows, 128), jnp.float32),
                pltpu.VMEM((rows, LAT), jnp.float32),
                dma((11,)),
                dma((3,)),
                dma((3,)),
                dma((1,)),
                dma((1,)),
                dma((3,)),
                dma((3,)),
            ]
            + [dma((2, 4, 3))] * 8
            + [
                pltpu.VMEM((depth, width), jnp.bfloat16),
                pltpu.VMEM((depth, width), jnp.bfloat16),
                pltpu.VMEM((2, width, depth), jnp.bfloat16),
                pltpu.VMEM((tokens, depth), jnp.bfloat16),
                pltpu.VMEM((tokens, depth), jnp.bfloat16),
                pltpu.VMEM((ys, cut, tokens), jnp.float32),
                pltpu.VMEM((2, 7, cut // 2, tokens), jnp.bfloat16),
                pltpu.VMEM((2, 7, cut // 2, tokens), jnp.bfloat16),
                dma((4,)),
                dma((4,)),
                dma((heads,)),
                dma((heads,)),
                dma((2, 7)),
                dma((2, 7)),
                pltpu.SMEM(chosen.shape, jnp.int32),
            ],
            compiler_params=pltpu.CompilerParams(
                collective_id=0, has_side_effects=True, vmem_limit_bytes=67043328
            ),
        )(q_nope, q_rope, latent, key_rope, chosen, w_uk, w_uv, w_out).T

    return jax.shard_map(
        on_device,
        mesh=mesh,
        in_specs=(
            P("ctx", "head"),
            P("ctx", "head"),
            P("ctx", None, None),
            P("ctx", None, None),
            P("ctx", None),
            P("head", None, None),
            P("head", None, None),
            P("head", None),
        ),
        out_specs=P("ctx", "head"),
        check_vma=False,
    )
```

```python
import math

import jax
import jax.numpy as jnp
from jax import lax
from jax.experimental import pallas as pl
from jax.experimental.pallas import tpu as pltpu
from jax.sharding import PartitionSpec as P

LAT = 512
ROPE = 64
QK_NOPE = 128
VHEAD = 128
BLOCK = 128
ROWS = 144
THIRD = 48
PIECES = 3
MASKED = -1e30
MESH = pl.DeviceIdType.MESH


def gather_attend(
    heads,
    planes,
    ys,
    q_nope,
    q_rope,
    latent,
    key_rope,
    chosen_hbm,
    w_uk,
    w_uv,
    w_out,
    out,
    kv,
    qn_buf,
    qr_buf,
    wuk_buf,
    wuv_buf,
    q_lat,
    q_rot,
    bias,
    row_max,
    row_sum,
    acc,
    load_sem,
    x_send,
    x_recv,
    own_send,
    own_recv,
    xp_send,
    xp_recv,
    z_send,
    z_recv,
    y_send,
    y_recv,
    zp_send,
    zp_recv,
    yp_send,
    yp_recv,
    w_mine,
    w_peer,
    w_turned,
    values,
    v_peer,
    piece,
    staged,
    landed,
    w_send,
    w_recv,
    v_send,
    v_recv,
    r_send,
    r_recv,
    chosen,
):
    ci = lax.axis_index("ctx")
    hi = lax.axis_index("head")
    z, xh, core = ci // 4, (ci // 2) % 2, ci % 2
    xl, y = hi // ys, hi % ys
    color = y % 2

    def ctx_at(zz):
        return lax.rem(zz + planes, planes) * 4 + xh * 2 + core

    def head_at(yy):
        return xl * ys + lax.rem(yy + ys, ys)

    partner = (z * 4 + xh * 2 + (1 - core), hi)
    across = (z * 4 + (1 - xh) * 2 + core, (1 - xl) * ys + y)
    beside = (ci, (1 - xl) * ys + y)
    z_next, z_prev = (ctx_at(z + 1), hi), (ctx_at(z - 1), hi)
    y_next, y_prev = (ci, head_at(y + 1)), (ci, head_at(y - 1))
    y_over, y_under = (ci, head_at(y + 2)), (ci, head_at(y - 2))
    toward_z = (z_next, z_prev)
    aslant = ((ctx_at(z + 1), head_at(y + 1)), (ctx_at(z - 1), head_at(y - 1)))
    toward_y = ((y_next, y_prev), (y_over, y_under))

    loads = [pltpu.make_async_copy(latent.at[0], kv.at[ci, 0:BLOCK, :], load_sem.at[0])]
    for i in range(4):
        loads.append(
            pltpu.make_async_copy(
                key_rope.at[0, 16 * i : 16 * i + 16, :],
                kv.at[ci, BLOCK:ROWS, 128 * i : 128 * i + 128],
                load_sem.at[1 + i],
            )
        )
    for i, (src, dst) in enumerate(
        ((q_nope, qn_buf), (w_uk, wuk_buf), (q_rope, qr_buf), (w_uv, wuv_buf))
    ):
        loads.append(pltpu.make_async_copy(src, dst, load_sem.at[5 + i]))
    width = w_mine.shape[1]
    cut = out.shape[0]
    quarter = w_mine.shape[0] // 4
    my_columns = pl.ds(pl.multiple_of(xl * width, width), width)
    peer_columns = pl.ds(pl.multiple_of((1 - xl) * width, width), width)
    loads.append(pltpu.make_async_copy(w_out.at[:, my_columns], w_mine, load_sem.at[9]))
    loads.append(pltpu.make_async_copy(chosen_hbm, chosen, load_sem.at[10]))
    for copy in loads:
        copy.start()

    barrier = pltpu.get_barrier_semaphore()
    greeted = (partner, across, beside) + toward_z + aslant + toward_y[0] + toward_y[1]
    for device in greeted:
        pl.semaphore_signal(barrier, inc=1, device_id=device, device_id_type=MESH)
    pl.semaphore_wait(barrier, len(greeted))

    def part(block, p):
        return kv.at[block, THIRD * p : THIRD * (p + 1), :]

    def send(block, p, send_sem, recv_sem, device):
        return pltpu.make_async_remote_copy(
            part(block, p), part(block, p), send_sem, recv_sem, device_id=device, device_id_type=MESH
        )

    def plane_of(d, hop):
        return lax.rem(z + planes - hop, planes) if d == 0 else lax.rem(z + hop, planes)

    def mine(plane):
        return plane * 4 + color * 2 + core

    def other(plane):
        return plane * 4 + (1 - color) * 2 + core

    def z_copy(d, hop, p):
        return send(
            mine(plane_of(d, hop - 1)), p, z_send.at[d, hop - 1, p], z_recv.at[d, hop - 1, p], toward_z[d]
        )

    def y_copy(d, hop, p):
        if hop == 4:
            return send(mine(plane_of(d, 3)), p, y_send.at[d, 3, p], y_recv.at[d, 3, p], aslant[d])
        return send(mine(plane_of(d, hop)), p, y_send.at[d, hop - 1, p], y_recv.at[d, hop - 1, p], toward_y[0][d])

    def y_arrival(d, hop, p):
        return send(other(plane_of(d, hop)), p, y_send.at[d, hop - 1, p], y_recv.at[d, hop - 1, p], toward_y[0][d])

    def zp_copy(d, hop, p):
        return send(mine(plane_of(d, hop)), p, zp_send.at[d, hop - 1, p], zp_recv.at[d, hop - 1, p], partner)

    def yp_copy(d, hop, p):
        return send(other(plane_of(d, hop)), p, yp_send.at[d, hop - 1, p], yp_recv.at[d, hop - 1, p], partner)

    def carried(d, hop, p):
        return hop < 4 or (p < 2 if d == 0 else p == 2)

    for copy in loads[:5]:
        copy.wait()
    across_block = z * 4 + (1 - xh) * 2 + core
    x_copies = [send(ci, p, x_send.at[p], x_recv.at[p], across) for p in range(PIECES)]
    for copy in x_copies:
        copy.start()
    own_copy = pltpu.make_async_remote_copy(
        kv.at[ci], kv.at[ci], own_send.at[0], own_recv.at[0], device_id=partner, device_id_type=MESH
    )
    own_copy.start()

    @pl.when(xh == color)
    def _():
        for p in range(PIECES):
            for d in range(2):
                z_copy(d, 1, p).start()

    def w_rows(which, of_core):
        return pl.ds(pl.multiple_of((2 * of_core + which) * quarter, quarter), quarter)

    w_copies = [
        pltpu.make_async_remote_copy(
            w_out.at[w_rows(which, core), peer_columns],
            w_peer.at[w_rows(which, core), :],
            w_send.at[which],
            w_recv.at[which],
            device_id=device,
            device_id_type=MESH,
        )
        for which, device in enumerate((beside, across))
    ]
    wp_copies = [
        pltpu.make_async_remote_copy(
            w_peer.at[w_rows(which, core), :],
            w_peer.at[w_rows(which, core), :],
            w_send.at[2 + which],
            w_recv.at[2 + which],
            device_id=partner,
            device_id_type=MESH,
        )
        for which in range(2)
    ]
    for copy in w_copies:
        copy.start()

    loads[10].wait()
    block_ids = lax.broadcasted_iota(jnp.int32, (planes * 4, BLOCK), 0)
    listed = block_ids < 0
    for j in range(chosen.shape[1]):
        listed = jnp.logical_or(listed, block_ids == chosen[0, j])
    bias[...] = jnp.where(listed, 0.0, MASKED)
    row_max[...] = jnp.full_like(row_max, MASKED)
    row_sum[...] = jnp.zeros_like(row_sum)
    acc[...] = jnp.zeros_like(acc)

    xp_copies = [send(across_block, p, xp_send.at[p], xp_recv.at[p], partner) for p in range(PIECES)]
    for p in range(PIECES):
        x_copies[p].wait_recv()
        xp_copies[p].start()

        @pl.when(xh != color)
        def _():
            for d in range(2):
                z_copy(d, 1, p).start()

    for copy in loads[5:8]:
        copy.wait()
    for h in range(heads):
        rows = slice(BLOCK * h, BLOCK * (h + 1))
        q_lat[rows, :] = jnp.dot(
            qn_buf[:, QK_NOPE * h : QK_NOPE * (h + 1)], wuk_buf[h], preferred_element_type=jnp.float32
        ).astype(jnp.bfloat16)
        q_rot[rows, :] = qr_buf[:, ROPE * h : ROPE * (h + 1)]

    scale = (QK_NOPE + ROPE) ** -0.5 * math.log2(math.e)
    half = heads * BLOCK // 2

    def attend(blocks, r, own=False):
        rows = slice(0, 2 * half) if r is None else slice(r * half, (r + 1) * half)
        keys = jnp.concatenate([kv[b, 0:BLOCK, :] for b in blocks], axis=0)
        rotary = jnp.concatenate(
            [
                jnp.concatenate([kv[b, BLOCK:ROWS, 128 * j : 128 * (j + 1)] for j in range(4)], axis=0)
                for b in blocks
            ],
            axis=1,
        )
        scores = lax.dot_general(
            q_lat[rows, :], keys, (((1,), (1,)), ((), ())), preferred_element_type=jnp.float32
        )
        scores = scores + jnp.dot(q_rot[rows, :], rotary, preferred_element_type=jnp.float32)
        hidden = jnp.concatenate([bias[pl.ds(b, 1), :] for b in blocks], axis=1)
        scores = scores * scale + hidden
        if own:
            t_ids = lax.broadcasted_iota(jnp.int32, scores.shape, 0) % BLOCK
            col_ids = lax.broadcasted_iota(jnp.int32, scores.shape, 1)
            u_ids = col_ids - (ci % 4) * BLOCK
            later = (u_ids > t_ids) & (u_ids < BLOCK)
            scores = jnp.where(later, MASKED, scores)
        old_max = row_max[rows, :]
        new_max = jnp.maximum(old_max, jnp.max(scores, axis=1, keepdims=True))
        factor = jnp.exp2(old_max - new_max)
        wide = jnp.concatenate([new_max] * len(blocks), axis=1)
        exponent = jnp.exp2(scores - wide)
        total = sum(exponent[:, 128 * i : 128 * (i + 1)] for i in range(1, len(blocks))) + exponent[:, 0:128]
        row_max[rows, :] = new_max
        row_sum[rows, :] = row_sum[rows, :] * factor + total
        acc[rows, :] = acc[rows, :] * jnp.concatenate([factor] * 4, axis=1) + jnp.dot(
            exponent.astype(jnp.bfloat16), keys, preferred_element_type=jnp.float32
        )

    def turn(source, which):
        for j in range(width // 128):
            columns = slice(128 * j, 128 * (j + 1))
            w_turned[which, columns, :] = source[:, columns].T

    both = range(2)

    def z_take(hop, p):
        for d in both:
            if carried(d, hop, p):
                z_copy(d, hop, p).wait_recv()
                for later in {1: (2,), 2: (3,), 3: (4,)}.get(hop, ()):
                    if carried(d, later, p):
                        z_copy(d, later, p).start()
                        if later == 4:
                            y_copy(d, 4, p).start()
        for d in both:
            if carried(d, hop, p):
                if hop < 4:
                    y_copy(d, hop, p).start()
                zp_copy(d, hop, p).start()

    def y_take(hop, p):
        for d in both:
            if carried(d, hop, p):
                y_arrival(d, hop, p).wait_recv()
                yp_copy(d, hop, p).start()

    def complete(d, hop, by_z):
        for p in range(PIECES):
            if carried(d, hop, p):
                (zp_copy if by_z else yp_copy)(d, hop, p).wait_recv()

    def chunk(hop, by_z):
        which = color if by_z else 1 - color
        for d in both:
            complete(d, hop, by_z)
        return [plane_of(d, hop) * 4 + which * 2 + i for d in both for i in range(2)]

    z_take(1, 0)
    own_copy.wait_recv()
    for p in range(PIECES):
        xp_copies[p].wait_recv()
    own_plane = [z * 4 + i for i in range(4)]
    attend(own_plane, 0, True)
    z_take(1, 1)
    attend(own_plane, 1, True)
    z_take(1, 2)
    blocks = chunk(1, True)
    attend(blocks, 0)
    z_take(2, 0)
    y_take(1, 0)
    attend(blocks, 1)
    z_take(2, 1)
    y_take(1, 1)
    loads[9].wait()
    turn(w_mine, 0)
    z_take(2, 2)
    y_take(1, 2)
    blocks = chunk(2, True)
    attend(blocks, 0)
    z_take(3, 0)
    y_take(2, 0)
    attend(blocks, 1)
    for copy in w_copies:
        copy.wait_recv()
    for copy in wp_copies:
        copy.start()
    z_take(3, 1)
    y_take(2, 1)
    blocks = chunk(1, False)
    attend(blocks, 0)
    z_take(3, 2)
    y_take(2, 2)
    attend(blocks, 1)
    for copy in wp_copies:
        copy.wait_recv()
    turn(w_peer, 1)
    blocks = chunk(2, False)
    attend(blocks, None)
    for p in range(PIECES):
        z_take(4, p)
        y_take(3, p)
    blocks = chunk(3, True)
    attend(blocks, None)
    for p in range(PIECES):
        y_take(4, p)
    blocks = chunk(3, False)
    attend(blocks, None)
    for d in both:
        for by_z in (True, False):
            complete(d, 4, by_z)
    blocks = [plane_of(0, 4) * 4 + i for i in range(4)]

    loads[8].wait()
    v_copies = []
    for r in range(2):
        attend(blocks, r)
        for h in range(heads // 2 * r, heads // 2 * (r + 1)):
            rows = slice(BLOCK * h, BLOCK * (h + 1))
            columns = slice(VHEAD * h, VHEAD * (h + 1))
            denominator = jnp.sum(row_sum[rows, :], axis=1, keepdims=True)
            mix = (acc[rows, :] / denominator).astype(jnp.bfloat16)
            values[:, columns] = jnp.dot(mix, wuv_buf[h], preferred_element_type=jnp.float32).astype(jnp.bfloat16)
            v_copies.append(
                pltpu.make_async_remote_copy(
                    values.at[:, columns],
                    v_peer.at[:, columns],
                    v_send.at[h],
                    v_recv.at[h],
                    device_id=beside,
                    device_id_type=MESH,
                )
            )
            v_copies[h].start()

    def owner(step):
        return lax.rem(y + step + 2 * ys, ys)

    def product(step, which, features):
        rows = pl.ds(pl.multiple_of(owner(step) * cut, 16), cut)
        return lax.dot_general(
            w_turned[which, rows, :],
            features[...],
            (((1,), (1,)), ((), ())),
            preferred_element_type=jnp.float32,
        )

    def own_part(step):
        piece[owner(step)] = product(step, 0, values)

    def peer_part(step):
        piece[owner(step)] += product(step, 1, v_peer)

    steps = [4, 3, -3, 1, -1, 2, -2, 0]
    for away in steps:
        own_part(away)
    for copy in v_copies:
        copy.wait_recv()

    rows_half = piece.shape[1] // 2
    sign = (1, -1)

    def r_copy(d, away, t):
        slot = {4: 0, 3: 1 + t, 1: 3 + t, 2: 5 + t}[away]
        stride = {4: 2, 3: 1, 1: 1, 2: 2}[away]
        return pltpu.make_async_remote_copy(
            staged.at[d, slot],
            landed.at[d, slot],
            r_send.at[d, slot],
            r_recv.at[d, slot],
            device_id=toward_y[stride - 1][d],
            device_id_type=MESH,
        )

    def take_sum(d, away, t):
        r_copy(d, away, t).wait_recv()
        return landed[d, {4: 0, 3: 1 + t, 1: 3 + t, 2: 5 + t}[away]].astype(jnp.float32)

    def send_sum(d, away, t):
        total = piece[owner(sign[d] * away), rows_half * t : rows_half * (t + 1), :]
        if away == 2:
            total = total + take_sum(d, 3, t)
            if t == d:
                total = total + take_sum(d, 4, t)
        staged[d, {4: 0, 3: 1 + t, 1: 3 + t, 2: 5 + t}[away]] = total.astype(jnp.bfloat16)
        r_copy(d, away, t).start()

    peer_part(4)
    for d in both:
        send_sum(d, 4, d)
    for away in (3, 1):
        for d in both:
            peer_part(sign[d] * away)
            for t in (d, 1 - d):
                send_sum(d, away, t)
    for away in (2, -2, 0):
        peer_part(away)
    for i in range(2):
        for d in both:
            send_sum(d, 2, (1 - d, d)[i])
    mine_of = [piece[owner(0), rows_half * t : rows_half * (t + 1), :] for t in range(2)]
    for t in range(2):
        for d in both:
            mine_of[t] = mine_of[t] + take_sum(d, 1, t)
    for t in range(2):
        for d in both:
            mine_of[t] = mine_of[t] + take_sum(d, 2, t)
        out[rows_half * t : rows_half * (t + 1), :] = mine_of[t].astype(jnp.bfloat16)

    for d in both:
        r_copy(d, 4, d).wait_send()
        for away in (3, 1, 2):
            for t in range(2):
                r_copy(d, away, t).wait_send()
    for copy in w_copies + wp_copies + v_copies:
        copy.wait_send()
    for copy in x_copies + xp_copies + [own_copy]:
        copy.wait_send()
    for d in range(2):
        for hop in range(1, 5):
            for p in range(PIECES):
                if carried(d, hop, p):
                    z_copy(d, hop, p).wait_send()
                    y_copy(d, hop, p).wait_send()
                    zp_copy(d, hop, p).wait_send()
                    yp_copy(d, hop, p).wait_send()


def solution(mesh):
    planes = mesh.shape["ctx"] // 4
    ys = mesh.shape["head"] // 2

    def on_device(q_nope, q_rope, latent, key_rope, chosen, w_uk, w_uv, w_out):
        heads = w_uk.shape[0]
        tokens = q_nope.shape[0]
        rows = heads * tokens
        anywhere = pl.BlockSpec(memory_space=pl.ANY)
        dma = pltpu.SemaphoreType.DMA

        def kernel(*refs):
            gather_attend(heads, planes, ys, *refs)

        depth = heads * VHEAD
        width = w_out.shape[1] // 2
        cut = width // ys
        return pl.pallas_call(
            kernel,
            out_shape=jax.ShapeDtypeStruct((cut, tokens), jnp.bfloat16),
            in_specs=[anywhere] * 8,
            out_specs=pl.BlockSpec(memory_space=pltpu.VMEM),
            scratch_shapes=[
                pltpu.VMEM((planes * 4, ROWS, LAT), jnp.bfloat16),
                pltpu.VMEM(q_nope.shape, jnp.bfloat16),
                pltpu.VMEM(q_rope.shape, jnp.bfloat16),
                pltpu.VMEM(w_uk.shape, jnp.bfloat16),
                pltpu.VMEM(w_uv.shape, jnp.bfloat16),
                pltpu.VMEM((rows, LAT), jnp.bfloat16),
                pltpu.VMEM((rows, ROPE), jnp.bfloat16),
                pltpu.VMEM((planes * 4, BLOCK), jnp.float32),
                pltpu.VMEM((rows, 128), jnp.float32),
                pltpu.VMEM((rows, 128), jnp.float32),
                pltpu.VMEM((rows, LAT), jnp.float32),
                dma((11,)),
                dma((3,)),
                dma((3,)),
                dma((1,)),
                dma((1,)),
                dma((3,)),
                dma((3,)),
            ]
            + [dma((2, 4, 3))] * 8
            + [
                pltpu.VMEM((depth, width), jnp.bfloat16),
                pltpu.VMEM((depth, width), jnp.bfloat16),
                pltpu.VMEM((2, width, depth), jnp.bfloat16),
                pltpu.VMEM((tokens, depth), jnp.bfloat16),
                pltpu.VMEM((tokens, depth), jnp.bfloat16),
                pltpu.VMEM((ys, cut, tokens), jnp.float32),
                pltpu.VMEM((2, 7, cut // 2, tokens), jnp.bfloat16),
                pltpu.VMEM((2, 7, cut // 2, tokens), jnp.bfloat16),
                dma((4,)),
                dma((4,)),
                dma((heads,)),
                dma((heads,)),
                dma((2, 7)),
                dma((2, 7)),
                pltpu.SMEM(chosen.shape, jnp.int32),
            ],
            compiler_params=pltpu.CompilerParams(
                collective_id=0, has_side_effects=True, vmem_limit_bytes=67043328
            ),
        )(q_nope, q_rope, latent, key_rope, chosen, w_uk, w_uv, w_out).T

    return jax.shard_map(
        on_device,
        mesh=mesh,
        in_specs=(
            P("ctx", "head"),
            P("ctx", "head"),
            P("ctx", None, None),
            P("ctx", None, None),
            P("ctx", None),
            P("head", None, None),
            P("head", None, None),
            P("head", None),
        ),
        out_specs=P("ctx", "head"),
        check_vma=False,
    )
```

```python
import math

import jax
import jax.numpy as jnp
from jax import lax
from jax.experimental import pallas as pl
from jax.experimental.pallas import tpu as pltpu
from jax.sharding import PartitionSpec as P

LAT = 512
ROPE = 64
QK_NOPE = 128
VHEAD = 128
BLOCK = 128
ROWS = 144
THIRD = 48
PIECES = 3
MASKED = -1e30
MESH = pl.DeviceIdType.MESH


def gather_attend(
    heads,
    planes,
    ys,
    q_nope,
    q_rope,
    latent,
    key_rope,
    chosen_hbm,
    w_uk,
    w_uv,
    w_out,
    out,
    kv,
    qn_buf,
    qr_buf,
    wuk_buf,
    wuv_buf,
    q_lat,
    q_rot,
    bias,
    row_max,
    row_sum,
    acc,
    load_sem,
    x_send,
    x_recv,
    own_send,
    own_recv,
    xp_send,
    xp_recv,
    z_send,
    z_recv,
    y_send,
    y_recv,
    zp_send,
    zp_recv,
    yp_send,
    yp_recv,
    w_mine,
    w_peer,
    w_turned,
    values,
    v_peer,
    piece,
    staged,
    landed,
    w_send,
    w_recv,
    v_send,
    v_recv,
    r_send,
    r_recv,
    chosen,
):
    ci = lax.axis_index("ctx")
    hi = lax.axis_index("head")
    z, xh, core = ci // 4, (ci // 2) % 2, ci % 2
    xl, y = hi // ys, hi % ys
    color = y % 2

    def ctx_at(zz):
        return lax.rem(zz + planes, planes) * 4 + xh * 2 + core

    def head_at(yy):
        return xl * ys + lax.rem(yy + ys, ys)

    partner = (z * 4 + xh * 2 + (1 - core), hi)
    across = (z * 4 + (1 - xh) * 2 + core, (1 - xl) * ys + y)
    beside = (ci, (1 - xl) * ys + y)
    z_next, z_prev = (ctx_at(z + 1), hi), (ctx_at(z - 1), hi)
    y_next, y_prev = (ci, head_at(y + 1)), (ci, head_at(y - 1))
    y_over, y_under = (ci, head_at(y + 2)), (ci, head_at(y - 2))
    toward_z = (z_next, z_prev)
    aslant = ((ctx_at(z + 1), head_at(y + 1)), (ctx_at(z - 1), head_at(y - 1)))
    toward_y = ((y_next, y_prev), (y_over, y_under))

    barrier = pltpu.get_barrier_semaphore()
    greeted = (partner, across, beside) + toward_z + aslant + toward_y[0] + toward_y[1]
    for device in greeted:
        pl.semaphore_signal(barrier, inc=1, device_id=device, device_id_type=MESH)

    loads = [pltpu.make_async_copy(latent.at[0], kv.at[ci, 0:BLOCK, :], load_sem.at[0])]
    for i in range(4):
        loads.append(
            pltpu.make_async_copy(
                key_rope.at[0, 16 * i : 16 * i + 16, :],
                kv.at[ci, BLOCK:ROWS, 128 * i : 128 * i + 128],
                load_sem.at[1 + i],
            )
        )
    for i, (src, dst) in enumerate(
        ((q_nope, qn_buf), (w_uk, wuk_buf), (q_rope, qr_buf), (w_uv, wuv_buf))
    ):
        loads.append(pltpu.make_async_copy(src, dst, load_sem.at[5 + i]))
    width = w_mine.shape[1]
    cut = out.shape[0]
    quarter = w_mine.shape[0] // 4
    my_columns = pl.ds(pl.multiple_of(xl * width, width), width)
    peer_columns = pl.ds(pl.multiple_of((1 - xl) * width, width), width)
    loads.append(pltpu.make_async_copy(w_out.at[:, my_columns], w_mine, load_sem.at[9]))
    loads.append(pltpu.make_async_copy(chosen_hbm, chosen, load_sem.at[10]))
    for copy in loads:
        copy.start()

    pl.semaphore_wait(barrier, len(greeted))

    def part(block, p):
        return kv.at[block, THIRD * p : THIRD * (p + 1), :]

    def send(block, p, send_sem, recv_sem, device):
        return pltpu.make_async_remote_copy(
            part(block, p), part(block, p), send_sem, recv_sem, device_id=device, device_id_type=MESH
        )

    def plane_of(d, hop):
        return lax.rem(z + planes - hop, planes) if d == 0 else lax.rem(z + hop, planes)

    def mine(plane):
        return plane * 4 + color * 2 + core

    def other(plane):
        return plane * 4 + (1 - color) * 2 + core

    def z_copy(d, hop, p):
        return send(
            mine(plane_of(d, hop - 1)), p, z_send.at[d, hop - 1, p], z_recv.at[d, hop - 1, p], toward_z[d]
        )

    def y_copy(d, hop, p):
        if hop == 4:
            return send(mine(plane_of(d, 3)), p, y_send.at[d, 3, p], y_recv.at[d, 3, p], aslant[d])
        return send(mine(plane_of(d, hop)), p, y_send.at[d, hop - 1, p], y_recv.at[d, hop - 1, p], toward_y[0][d])

    def y_arrival(d, hop, p):
        return send(other(plane_of(d, hop)), p, y_send.at[d, hop - 1, p], y_recv.at[d, hop - 1, p], toward_y[0][d])

    def zp_copy(d, hop, p):
        return send(mine(plane_of(d, hop)), p, zp_send.at[d, hop - 1, p], zp_recv.at[d, hop - 1, p], partner)

    def yp_copy(d, hop, p):
        return send(other(plane_of(d, hop)), p, yp_send.at[d, hop - 1, p], yp_recv.at[d, hop - 1, p], partner)

    def carried(d, hop, p):
        return hop < 4 or (p < 2 if d == 0 else p == 2)

    for copy in loads[:5]:
        copy.wait()
    across_block = z * 4 + (1 - xh) * 2 + core
    x_copies = [send(ci, p, x_send.at[p], x_recv.at[p], across) for p in range(PIECES)]
    for copy in x_copies:
        copy.start()
    own_copy = pltpu.make_async_remote_copy(
        kv.at[ci], kv.at[ci], own_send.at[0], own_recv.at[0], device_id=partner, device_id_type=MESH
    )
    own_copy.start()

    @pl.when(xh == color)
    def _():
        for p in range(PIECES):
            for d in range(2):
                z_copy(d, 1, p).start()

    def w_rows(which, of_core):
        return pl.ds(pl.multiple_of((2 * of_core + which) * quarter, quarter), quarter)

    w_copies = [
        pltpu.make_async_remote_copy(
            w_out.at[w_rows(which, core), peer_columns],
            w_peer.at[w_rows(which, core), :],
            w_send.at[which],
            w_recv.at[which],
            device_id=device,
            device_id_type=MESH,
        )
        for which, device in enumerate((beside, across))
    ]
    wp_copies = [
        pltpu.make_async_remote_copy(
            w_peer.at[w_rows(which, core), :],
            w_peer.at[w_rows(which, core), :],
            w_send.at[2 + which],
            w_recv.at[2 + which],
            device_id=partner,
            device_id_type=MESH,
        )
        for which in range(2)
    ]
    for copy in w_copies:
        copy.start()

    loads[10].wait()
    block_ids = lax.broadcasted_iota(jnp.int32, (planes * 4, BLOCK), 0)
    listed = block_ids < 0
    for j in range(chosen.shape[1]):
        listed = jnp.logical_or(listed, block_ids == chosen[0, j])
    bias[...] = jnp.where(listed, 0.0, MASKED)
    row_max[...] = jnp.full_like(row_max, MASKED)
    row_sum[...] = jnp.zeros_like(row_sum)
    acc[...] = jnp.zeros_like(acc)

    xp_copies = [send(across_block, p, xp_send.at[p], xp_recv.at[p], partner) for p in range(PIECES)]
    for p in range(PIECES):
        x_copies[p].wait_recv()
        xp_copies[p].start()

        @pl.when(xh != color)
        def _():
            for d in range(2):
                z_copy(d, 1, p).start()

    for copy in loads[5:8]:
        copy.wait()
    for h in range(heads):
        rows = slice(BLOCK * h, BLOCK * (h + 1))
        q_lat[rows, :] = jnp.dot(
            qn_buf[:, QK_NOPE * h : QK_NOPE * (h + 1)], wuk_buf[h], preferred_element_type=jnp.float32
        ).astype(jnp.bfloat16)
        q_rot[rows, :] = qr_buf[:, ROPE * h : ROPE * (h + 1)]

    scale = (QK_NOPE + ROPE) ** -0.5 * math.log2(math.e)
    half = heads * BLOCK // 2

    def attend(blocks, r, own=False):
        rows = slice(0, 2 * half) if r is None else slice(r * half, (r + 1) * half)
        keys = jnp.concatenate([kv[b, 0:BLOCK, :] for b in blocks], axis=0)
        rotary = jnp.concatenate(
            [
                jnp.concatenate([kv[b, BLOCK:ROWS, 128 * j : 128 * (j + 1)] for j in range(4)], axis=0)
                for b in blocks
            ],
            axis=1,
        )
        scores = lax.dot_general(
            q_lat[rows, :], keys, (((1,), (1,)), ((), ())), preferred_element_type=jnp.float32
        )
        scores = scores + jnp.dot(q_rot[rows, :], rotary, preferred_element_type=jnp.float32)
        hidden = jnp.concatenate([bias[pl.ds(b, 1), :] for b in blocks], axis=1)
        scores = scores * scale + hidden
        if own:
            t_ids = lax.broadcasted_iota(jnp.int32, scores.shape, 0) % BLOCK
            col_ids = lax.broadcasted_iota(jnp.int32, scores.shape, 1)
            u_ids = col_ids - (ci % 4) * BLOCK
            later = (u_ids > t_ids) & (u_ids < BLOCK)
            scores = jnp.where(later, MASKED, scores)
        old_max = row_max[rows, :]
        new_max = jnp.maximum(old_max, jnp.max(scores, axis=1, keepdims=True))
        factor = jnp.exp2(old_max - new_max)
        wide = jnp.concatenate([new_max] * len(blocks), axis=1)
        exponent = jnp.exp2(scores - wide)
        total = sum(exponent[:, 128 * i : 128 * (i + 1)] for i in range(1, len(blocks))) + exponent[:, 0:128]
        row_max[rows, :] = new_max
        row_sum[rows, :] = row_sum[rows, :] * factor + total
        acc[rows, :] = acc[rows, :] * jnp.concatenate([factor] * 4, axis=1) + jnp.dot(
            exponent.astype(jnp.bfloat16), keys, preferred_element_type=jnp.float32
        )

    def turn(source, which):
        for j in range(width // 128):
            columns = slice(128 * j, 128 * (j + 1))
            w_turned[which, columns, :] = source[:, columns].T

    both = range(2)

    def z_take(hop, p):
        for d in both:
            if carried(d, hop, p):
                z_copy(d, hop, p).wait_recv()
                for later in {1: (2,), 2: (3,), 3: (4,)}.get(hop, ()):
                    if carried(d, later, p):
                        z_copy(d, later, p).start()
                        if later == 4:
                            y_copy(d, 4, p).start()
        for d in both:
            if carried(d, hop, p):
                if hop < 4:
                    y_copy(d, hop, p).start()
                zp_copy(d, hop, p).start()

    def y_take(hop, p):
        for d in both:
            if carried(d, hop, p):
                y_arrival(d, hop, p).wait_recv()
                yp_copy(d, hop, p).start()

    def complete(d, hop, by_z):
        for p in range(PIECES):
            if carried(d, hop, p):
                (zp_copy if by_z else yp_copy)(d, hop, p).wait_recv()

    def chunk(hop, by_z):
        which = color if by_z else 1 - color
        for d in both:
            complete(d, hop, by_z)
        return [plane_of(d, hop) * 4 + which * 2 + i for d in both for i in range(2)]

    z_take(1, 0)
    own_copy.wait_recv()
    for p in range(PIECES):
        xp_copies[p].wait_recv()
    own_plane = [z * 4 + i for i in range(4)]
    attend(own_plane, 0, True)
    z_take(1, 1)
    attend(own_plane, 1, True)
    z_take(1, 2)
    blocks = chunk(1, True)
    attend(blocks, 0)
    z_take(2, 0)
    y_take(1, 0)
    attend(blocks, 1)
    z_take(2, 1)
    y_take(1, 1)
    loads[9].wait()
    turn(w_mine, 0)
    z_take(2, 2)
    y_take(1, 2)
    blocks = chunk(2, True)
    attend(blocks, 0)
    z_take(3, 0)
    y_take(2, 0)
    attend(blocks, 1)
    for copy in w_copies:
        copy.wait_recv()
    for copy in wp_copies:
        copy.start()
    z_take(3, 1)
    y_take(2, 1)
    blocks = chunk(1, False)
    attend(blocks, 0)
    z_take(3, 2)
    y_take(2, 2)
    attend(blocks, 1)
    for copy in wp_copies:
        copy.wait_recv()
    turn(w_peer, 1)
    blocks = chunk(2, False)
    attend(blocks, None)
    for p in range(PIECES):
        z_take(4, p)
        y_take(3, p)
    blocks = chunk(3, True)
    attend(blocks, None)
    for p in range(PIECES):
        y_take(4, p)
    blocks = chunk(3, False)
    attend(blocks, None)
    for d in both:
        for by_z in (True, False):
            complete(d, 4, by_z)
    blocks = [plane_of(0, 4) * 4 + i for i in range(4)]

    loads[8].wait()
    v_copies = []
    for r in range(2):
        attend(blocks, r)
        for h in range(heads // 2 * r, heads // 2 * (r + 1)):
            rows = slice(BLOCK * h, BLOCK * (h + 1))
            columns = slice(VHEAD * h, VHEAD * (h + 1))
            denominator = jnp.sum(row_sum[rows, :], axis=1, keepdims=True)
            mix = (acc[rows, :] / denominator).astype(jnp.bfloat16)
            values[:, columns] = jnp.dot(mix, wuv_buf[h], preferred_element_type=jnp.float32).astype(jnp.bfloat16)
            v_copies.append(
                pltpu.make_async_remote_copy(
                    values.at[:, columns],
                    v_peer.at[:, columns],
                    v_send.at[h],
                    v_recv.at[h],
                    device_id=beside,
                    device_id_type=MESH,
                )
            )
            v_copies[h].start()

    def owner(step):
        return lax.rem(y + step + 2 * ys, ys)

    def product(step, which, features):
        rows = pl.ds(pl.multiple_of(owner(step) * cut, 16), cut)
        return lax.dot_general(
            w_turned[which, rows, :],
            features[...],
            (((1,), (1,)), ((), ())),
            preferred_element_type=jnp.float32,
        )

    def own_part(step):
        piece[owner(step)] = product(step, 0, values)

    def peer_part(step):
        piece[owner(step)] += product(step, 1, v_peer)

    steps = [4, 3, -3, 1, -1, 2, -2, 0]
    for away in steps:
        own_part(away)
    for copy in v_copies:
        copy.wait_recv()

    rows_half = piece.shape[1] // 2
    sign = (1, -1)

    def r_copy(d, away, t):
        slot = {4: 0, 3: 1 + t, 1: 3 + t, 2: 5 + t}[away]
        stride = {4: 2, 3: 1, 1: 1, 2: 2}[away]
        return pltpu.make_async_remote_copy(
            staged.at[d, slot],
            landed.at[d, slot],
            r_send.at[d, slot],
            r_recv.at[d, slot],
            device_id=toward_y[stride - 1][d],
            device_id_type=MESH,
        )

    def take_sum(d, away, t):
        r_copy(d, away, t).wait_recv()
        return landed[d, {4: 0, 3: 1 + t, 1: 3 + t, 2: 5 + t}[away]].astype(jnp.float32)

    def send_sum(d, away, t):
        total = piece[owner(sign[d] * away), rows_half * t : rows_half * (t + 1), :]
        if away == 2:
            total = total + take_sum(d, 3, t)
            if t == d:
                total = total + take_sum(d, 4, t)
        staged[d, {4: 0, 3: 1 + t, 1: 3 + t, 2: 5 + t}[away]] = total.astype(jnp.bfloat16)
        r_copy(d, away, t).start()

    peer_part(4)
    for d in both:
        send_sum(d, 4, d)
    for away in (3, 1):
        for d in both:
            peer_part(sign[d] * away)
            for t in (d, 1 - d):
                send_sum(d, away, t)
    for away in (2, -2, 0):
        peer_part(away)
    for i in range(2):
        for d in both:
            send_sum(d, 2, (1 - d, d)[i])
    for copy in w_copies + wp_copies + v_copies:
        copy.wait_send()
    for copy in x_copies + xp_copies + [own_copy]:
        copy.wait_send()
    for d in range(2):
        for hop in range(1, 5):
            for p in range(PIECES):
                if carried(d, hop, p):
                    z_copy(d, hop, p).wait_send()
                    y_copy(d, hop, p).wait_send()
                    zp_copy(d, hop, p).wait_send()
                    yp_copy(d, hop, p).wait_send()

    mine_of = [piece[owner(0), rows_half * t : rows_half * (t + 1), :] for t in range(2)]
    for t in range(2):
        for d in both:
            mine_of[t] = mine_of[t] + take_sum(d, 1, t)
    for t in range(2):
        for d in both:
            mine_of[t] = mine_of[t] + take_sum(d, 2, t)
        out[rows_half * t : rows_half * (t + 1), :] = mine_of[t].astype(jnp.bfloat16)

    for d in both:
        r_copy(d, 4, d).wait_send()
        for away in (3, 1, 2):
            for t in range(2):
                r_copy(d, away, t).wait_send()


def solution(mesh):
    planes = mesh.shape["ctx"] // 4
    ys = mesh.shape["head"] // 2

    def on_device(q_nope, q_rope, latent, key_rope, chosen, w_uk, w_uv, w_out):
        heads = w_uk.shape[0]
        tokens = q_nope.shape[0]
        rows = heads * tokens
        anywhere = pl.BlockSpec(memory_space=pl.ANY)
        dma = pltpu.SemaphoreType.DMA

        def kernel(*refs):
            gather_attend(heads, planes, ys, *refs)

        depth = heads * VHEAD
        width = w_out.shape[1] // 2
        cut = width // ys
        return pl.pallas_call(
            kernel,
            out_shape=jax.ShapeDtypeStruct((cut, tokens), jnp.bfloat16),
            in_specs=[anywhere] * 8,
            out_specs=pl.BlockSpec(memory_space=pltpu.VMEM),
            scratch_shapes=[
                pltpu.VMEM((planes * 4, ROWS, LAT), jnp.bfloat16),
                pltpu.VMEM(q_nope.shape, jnp.bfloat16),
                pltpu.VMEM(q_rope.shape, jnp.bfloat16),
                pltpu.VMEM(w_uk.shape, jnp.bfloat16),
                pltpu.VMEM(w_uv.shape, jnp.bfloat16),
                pltpu.VMEM((rows, LAT), jnp.bfloat16),
                pltpu.VMEM((rows, ROPE), jnp.bfloat16),
                pltpu.VMEM((planes * 4, BLOCK), jnp.float32),
                pltpu.VMEM((rows, 128), jnp.float32),
                pltpu.VMEM((rows, 128), jnp.float32),
                pltpu.VMEM((rows, LAT), jnp.float32),
                dma((11,)),
                dma((3,)),
                dma((3,)),
                dma((1,)),
                dma((1,)),
                dma((3,)),
                dma((3,)),
            ]
            + [dma((2, 4, 3))] * 8
            + [
                pltpu.VMEM((depth, width), jnp.bfloat16),
                pltpu.VMEM((depth, width), jnp.bfloat16),
                pltpu.VMEM((2, width, depth), jnp.bfloat16),
                pltpu.VMEM((tokens, depth), jnp.bfloat16),
                pltpu.VMEM((tokens, depth), jnp.bfloat16),
                pltpu.VMEM((ys, cut, tokens), jnp.float32),
                pltpu.VMEM((2, 7, cut // 2, tokens), jnp.bfloat16),
                pltpu.VMEM((2, 7, cut // 2, tokens), jnp.bfloat16),
                dma((4,)),
                dma((4,)),
                dma((heads,)),
                dma((heads,)),
                dma((2, 7)),
                dma((2, 7)),
                pltpu.SMEM(chosen.shape, jnp.int32),
            ],
            compiler_params=pltpu.CompilerParams(
                collective_id=0, has_side_effects=True, vmem_limit_bytes=67043328
            ),
        )(q_nope, q_rope, latent, key_rope, chosen, w_uk, w_uv, w_out).T

    return jax.shard_map(
        on_device,
        mesh=mesh,
        in_specs=(
            P("ctx", "head"),
            P("ctx", "head"),
            P("ctx", None, None),
            P("ctx", None, None),
            P("ctx", None),
            P("head", None, None),
            P("head", None, None),
            P("head", None),
        ),
        out_specs=P("ctx", "head"),
        check_vma=False,
    )
```

```python
import math

import jax
import jax.numpy as jnp
from jax import lax
from jax.experimental import pallas as pl
from jax.experimental.pallas import tpu as pltpu
from jax.sharding import PartitionSpec as P

LAT = 512
ROPE = 64
QK_NOPE = 128
VHEAD = 128
BLOCK = 128
ROWS = 144
THIRD = 48
PIECES = 3
MASKED = -1e30
MESH = pl.DeviceIdType.MESH


def gather_attend(
    heads,
    planes,
    ys,
    q_nope,
    q_rope,
    latent,
    key_rope,
    chosen_hbm,
    w_uk,
    w_uv,
    w_out,
    out,
    kv,
    qn_buf,
    qr_buf,
    wuk_buf,
    wuv_buf,
    q_lat,
    q_rot,
    bias,
    row_max,
    row_sum,
    acc,
    load_sem,
    x_send,
    x_recv,
    own_send,
    own_recv,
    xp_send,
    xp_recv,
    z_send,
    z_recv,
    y_send,
    y_recv,
    zp_send,
    zp_recv,
    yp_send,
    yp_recv,
    w_mine,
    w_peer,
    w_turned,
    values,
    v_peer,
    piece,
    staged,
    landed,
    w_send,
    w_recv,
    v_send,
    v_recv,
    r_send,
    r_recv,
    chosen,
):
    ci = lax.axis_index("ctx")
    hi = lax.axis_index("head")
    z, xh, core = ci // 4, (ci // 2) % 2, ci % 2
    xl, y = hi // ys, hi % ys
    color = y % 2

    def ctx_at(zz):
        return lax.rem(zz + planes, planes) * 4 + xh * 2 + core

    def head_at(yy):
        return xl * ys + lax.rem(yy + ys, ys)

    partner = (z * 4 + xh * 2 + (1 - core), hi)
    across = (z * 4 + (1 - xh) * 2 + core, (1 - xl) * ys + y)
    beside = (ci, (1 - xl) * ys + y)
    z_next, z_prev = (ctx_at(z + 1), hi), (ctx_at(z - 1), hi)
    y_next, y_prev = (ci, head_at(y + 1)), (ci, head_at(y - 1))
    y_over, y_under = (ci, head_at(y + 2)), (ci, head_at(y - 2))
    toward_z = (z_next, z_prev)
    aslant = ((ctx_at(z + 1), head_at(y + 1)), (ctx_at(z - 1), head_at(y - 1)))
    toward_y = ((y_next, y_prev), (y_over, y_under))

    barrier = pltpu.get_barrier_semaphore()
    greeted = (partner, across, beside) + toward_z + aslant + toward_y[0] + toward_y[1]
    for device in greeted:
        pl.semaphore_signal(barrier, inc=1, device_id=device, device_id_type=MESH)

    loads = [pltpu.make_async_copy(latent.at[0], kv.at[ci, 0:BLOCK, :], load_sem.at[0])]
    for i in range(4):
        loads.append(
            pltpu.make_async_copy(
                key_rope.at[0, 16 * i : 16 * i + 16, :],
                kv.at[ci, BLOCK:ROWS, 128 * i : 128 * i + 128],
                load_sem.at[1 + i],
            )
        )
    for i, (src, dst) in enumerate(
        ((q_nope, qn_buf), (w_uk, wuk_buf), (q_rope, qr_buf), (w_uv, wuv_buf))
    ):
        loads.append(pltpu.make_async_copy(src, dst, load_sem.at[5 + i]))
    width = w_mine.shape[1]
    cut = out.shape[0]
    quarter = w_mine.shape[0] // 4
    my_columns = pl.ds(pl.multiple_of(xl * width, width), width)
    peer_columns = pl.ds(pl.multiple_of((1 - xl) * width, width), width)
    loads.append(pltpu.make_async_copy(w_out.at[:, my_columns], w_mine, load_sem.at[9]))
    loads.append(pltpu.make_async_copy(chosen_hbm, chosen, load_sem.at[10]))
    for copy in loads:
        copy.start()

    pl.semaphore_wait(barrier, len(greeted))

    def part(block, p):
        return kv.at[block, THIRD * p : THIRD * (p + 1), :]

    def send(block, p, send_sem, recv_sem, device):
        return pltpu.make_async_remote_copy(
            part(block, p), part(block, p), send_sem, recv_sem, device_id=device, device_id_type=MESH
        )

    def plane_of(d, hop):
        return lax.rem(z + planes - hop, planes) if d == 0 else lax.rem(z + hop, planes)

    def mine(plane):
        return plane * 4 + color * 2 + core

    def other(plane):
        return plane * 4 + (1 - color) * 2 + core

    def z_copy(d, hop, p):
        return send(
            mine(plane_of(d, hop - 1)), p, z_send.at[d, hop - 1, p], z_recv.at[d, hop - 1, p], toward_z[d]
        )

    def y_copy(d, hop, p):
        if hop == 4:
            return send(mine(plane_of(d, 3)), p, y_send.at[d, 3, p], y_recv.at[d, 3, p], aslant[d])
        return send(mine(plane_of(d, hop)), p, y_send.at[d, hop - 1, p], y_recv.at[d, hop - 1, p], toward_y[0][d])

    def y_arrival(d, hop, p):
        return send(other(plane_of(d, hop)), p, y_send.at[d, hop - 1, p], y_recv.at[d, hop - 1, p], toward_y[0][d])

    def zp_copy(d, hop, p):
        return send(mine(plane_of(d, hop)), p, zp_send.at[d, hop - 1, p], zp_recv.at[d, hop - 1, p], partner)

    def yp_copy(d, hop, p):
        return send(other(plane_of(d, hop)), p, yp_send.at[d, hop - 1, p], yp_recv.at[d, hop - 1, p], partner)

    def carried(d, hop, p):
        return hop < 4 or (p < 2 if d == 0 else p == 2)

    for copy in loads[:5]:
        copy.wait()
    across_block = z * 4 + (1 - xh) * 2 + core
    x_copies = [send(ci, p, x_send.at[p], x_recv.at[p], across) for p in range(PIECES)]
    for copy in x_copies:
        copy.start()
    own_copy = pltpu.make_async_remote_copy(
        kv.at[ci], kv.at[ci], own_send.at[0], own_recv.at[0], device_id=partner, device_id_type=MESH
    )
    own_copy.start()

    @pl.when(xh == color)
    def _():
        for p in range(PIECES):
            for d in range(2):
                z_copy(d, 1, p).start()

    def w_rows(which, of_core):
        return pl.ds(pl.multiple_of((2 * of_core + which) * quarter, quarter), quarter)

    w_copies = [
        pltpu.make_async_remote_copy(
            w_out.at[w_rows(which, core), peer_columns],
            w_peer.at[w_rows(which, core), :],
            w_send.at[which],
            w_recv.at[which],
            device_id=device,
            device_id_type=MESH,
        )
        for which, device in enumerate((beside, across))
    ]
    wp_copies = [
        pltpu.make_async_remote_copy(
            w_peer.at[w_rows(which, core), :],
            w_peer.at[w_rows(which, core), :],
            w_send.at[2 + which],
            w_recv.at[2 + which],
            device_id=partner,
            device_id_type=MESH,
        )
        for which in range(2)
    ]
    for copy in w_copies:
        copy.start()

    loads[10].wait()
    block_ids = lax.broadcasted_iota(jnp.int32, (planes * 4, BLOCK), 0)
    listed = block_ids < 0
    for j in range(chosen.shape[1]):
        listed = jnp.logical_or(listed, block_ids == chosen[0, j])
    bias[...] = jnp.where(listed, 0.0, MASKED)
    row_max[...] = jnp.full_like(row_max, MASKED)
    row_sum[...] = jnp.zeros_like(row_sum)
    acc[...] = jnp.zeros_like(acc)

    xp_copies = [send(across_block, p, xp_send.at[p], xp_recv.at[p], partner) for p in range(PIECES)]
    for p in range(PIECES):
        x_copies[p].wait_recv()

        @pl.when(xh != color)
        def _():
            for d in range(2):
                z_copy(d, 1, p).start()

        xp_copies[p].start()

    for copy in loads[5:8]:
        copy.wait()
    for h in range(heads):
        rows = slice(BLOCK * h, BLOCK * (h + 1))
        q_lat[rows, :] = jnp.dot(
            qn_buf[:, QK_NOPE * h : QK_NOPE * (h + 1)], wuk_buf[h], preferred_element_type=jnp.float32
        ).astype(jnp.bfloat16)
        q_rot[rows, :] = qr_buf[:, ROPE * h : ROPE * (h + 1)]

    scale = (QK_NOPE + ROPE) ** -0.5 * math.log2(math.e)
    half = heads * BLOCK // 2

    def attend(blocks, r, own=False):
        rows = slice(0, 2 * half) if r is None else slice(r * half, (r + 1) * half)
        keys = jnp.concatenate([kv[b, 0:BLOCK, :] for b in blocks], axis=0)
        rotary = jnp.concatenate(
            [
                jnp.concatenate([kv[b, BLOCK:ROWS, 128 * j : 128 * (j + 1)] for j in range(4)], axis=0)
                for b in blocks
            ],
            axis=1,
        )
        scores = lax.dot_general(
            q_lat[rows, :], keys, (((1,), (1,)), ((), ())), preferred_element_type=jnp.float32
        )
        scores = scores + jnp.dot(q_rot[rows, :], rotary, preferred_element_type=jnp.float32)
        hidden = jnp.concatenate([bias[pl.ds(b, 1), :] for b in blocks], axis=1)
        scores = scores * scale + hidden
        if own:
            t_ids = lax.broadcasted_iota(jnp.int32, scores.shape, 0) % BLOCK
            col_ids = lax.broadcasted_iota(jnp.int32, scores.shape, 1)
            u_ids = col_ids - (ci % 4) * BLOCK
            later = (u_ids > t_ids) & (u_ids < BLOCK)
            scores = jnp.where(later, MASKED, scores)
        old_max = row_max[rows, :]
        new_max = jnp.maximum(old_max, jnp.max(scores, axis=1, keepdims=True))
        factor = jnp.exp2(old_max - new_max)
        wide = jnp.concatenate([new_max] * len(blocks), axis=1)
        exponent = jnp.exp2(scores - wide)
        total = sum(exponent[:, 128 * i : 128 * (i + 1)] for i in range(1, len(blocks))) + exponent[:, 0:128]
        row_max[rows, :] = new_max
        row_sum[rows, :] = row_sum[rows, :] * factor + total
        acc[rows, :] = acc[rows, :] * jnp.concatenate([factor] * 4, axis=1) + jnp.dot(
            exponent.astype(jnp.bfloat16), keys, preferred_element_type=jnp.float32
        )

    def turn(source, which):
        for j in range(width // 128):
            columns = slice(128 * j, 128 * (j + 1))
            w_turned[which, columns, :] = source[:, columns].T

    both = range(2)

    def z_take(hop, p):
        for d in both:
            if carried(d, hop, p):
                z_copy(d, hop, p).wait_recv()
                for later in {1: (2,), 2: (3,), 3: (4,)}.get(hop, ()):
                    if carried(d, later, p):
                        z_copy(d, later, p).start()
                        if later == 4:
                            y_copy(d, 4, p).start()
        for d in both:
            if carried(d, hop, p):
                if hop < 4:
                    y_copy(d, hop, p).start()
                zp_copy(d, hop, p).start()

    def y_take(hop, p):
        for d in both:
            if carried(d, hop, p):
                y_arrival(d, hop, p).wait_recv()
                yp_copy(d, hop, p).start()

    def complete(d, hop, by_z):
        for p in range(PIECES):
            if carried(d, hop, p):
                (zp_copy if by_z else yp_copy)(d, hop, p).wait_recv()

    def chunk(hop, by_z):
        which = color if by_z else 1 - color
        for d in both:
            complete(d, hop, by_z)
        return [plane_of(d, hop) * 4 + which * 2 + i for d in both for i in range(2)]

    z_take(1, 0)
    own_copy.wait_recv()
    for p in range(PIECES):
        xp_copies[p].wait_recv()
    own_plane = [z * 4 + i for i in range(4)]
    attend(own_plane, 0, True)
    z_take(1, 1)
    attend(own_plane, 1, True)
    z_take(1, 2)
    blocks = chunk(1, True)
    attend(blocks, 0)
    z_take(2, 0)
    y_take(1, 0)
    attend(blocks, 1)
    z_take(2, 1)
    y_take(1, 1)
    loads[9].wait()
    turn(w_mine, 0)
    z_take(2, 2)
    y_take(1, 2)
    blocks = chunk(2, True)
    attend(blocks, 0)
    z_take(3, 0)
    y_take(2, 0)
    attend(blocks, 1)
    for copy in w_copies:
        copy.wait_recv()
    for copy in wp_copies:
        copy.start()
    z_take(3, 1)
    y_take(2, 1)
    blocks = chunk(1, False)
    attend(blocks, 0)
    z_take(3, 2)
    y_take(2, 2)
    attend(blocks, 1)
    for copy in wp_copies:
        copy.wait_recv()
    turn(w_peer, 1)
    blocks = chunk(2, False)
    attend(blocks, None)
    for p in range(PIECES):
        z_take(4, p)
        y_take(3, p)
    blocks = chunk(3, True)
    attend(blocks, None)
    for p in range(PIECES):
        y_take(4, p)
    blocks = chunk(3, False)
    attend(blocks, None)
    for d in both:
        for by_z in (True, False):
            complete(d, 4, by_z)
    blocks = [plane_of(0, 4) * 4 + i for i in range(4)]

    loads[8].wait()
    v_copies = []
    for r in range(2):
        attend(blocks, r)
        for h in range(heads // 2 * r, heads // 2 * (r + 1)):
            rows = slice(BLOCK * h, BLOCK * (h + 1))
            columns = slice(VHEAD * h, VHEAD * (h + 1))
            denominator = jnp.sum(row_sum[rows, :], axis=1, keepdims=True)
            mix = (acc[rows, :] / denominator).astype(jnp.bfloat16)
            values[:, columns] = jnp.dot(mix, wuv_buf[h], preferred_element_type=jnp.float32).astype(jnp.bfloat16)
            v_copies.append(
                pltpu.make_async_remote_copy(
                    values.at[:, columns],
                    v_peer.at[:, columns],
                    v_send.at[h],
                    v_recv.at[h],
                    device_id=beside,
                    device_id_type=MESH,
                )
            )
            v_copies[h].start()

    def owner(step):
        return lax.rem(y + step + 2 * ys, ys)

    def product(step, which, features):
        rows = pl.ds(pl.multiple_of(owner(step) * cut, 16), cut)
        return lax.dot_general(
            w_turned[which, rows, :],
            features[...],
            (((1,), (1,)), ((), ())),
            preferred_element_type=jnp.float32,
        )

    def own_part(step):
        piece[owner(step)] = product(step, 0, values)

    def peer_part(step):
        piece[owner(step)] += product(step, 1, v_peer)

    steps = [4, 3, -3, 1, -1, 2, -2, 0]
    for away in steps:
        own_part(away)
    for copy in v_copies:
        copy.wait_recv()

    rows_half = piece.shape[1] // 2
    sign = (1, -1)

    def r_copy(d, away, t):
        slot = {4: 0, 3: 1 + t, 1: 3 + t, 2: 5 + t}[away]
        stride = {4: 2, 3: 1, 1: 1, 2: 2}[away]
        return pltpu.make_async_remote_copy(
            staged.at[d, slot],
            landed.at[d, slot],
            r_send.at[d, slot],
            r_recv.at[d, slot],
            device_id=toward_y[stride - 1][d],
            device_id_type=MESH,
        )

    def take_sum(d, away, t):
        r_copy(d, away, t).wait_recv()
        return landed[d, {4: 0, 3: 1 + t, 1: 3 + t, 2: 5 + t}[away]].astype(jnp.float32)

    def send_sum(d, away, t):
        total = piece[owner(sign[d] * away), rows_half * t : rows_half * (t + 1), :]
        if away == 2:
            total = total + take_sum(d, 3, t)
            if t == d:
                total = total + take_sum(d, 4, t)
        staged[d, {4: 0, 3: 1 + t, 1: 3 + t, 2: 5 + t}[away]] = total.astype(jnp.bfloat16)
        r_copy(d, away, t).start()

    peer_part(4)
    for d in both:
        send_sum(d, 4, d)
    for away in (3, 1):
        for d in both:
            peer_part(sign[d] * away)
            for t in (d, 1 - d):
                send_sum(d, away, t)
    for away in (2, -2, 0):
        peer_part(away)
    for i in range(2):
        for d in both:
            send_sum(d, 2, (1 - d, d)[i])
    for copy in w_copies + wp_copies + v_copies:
        copy.wait_send()
    for copy in x_copies + xp_copies + [own_copy]:
        copy.wait_send()
    for d in range(2):
        for hop in range(1, 5):
            for p in range(PIECES):
                if carried(d, hop, p):
                    z_copy(d, hop, p).wait_send()
                    y_copy(d, hop, p).wait_send()
                    zp_copy(d, hop, p).wait_send()
                    yp_copy(d, hop, p).wait_send()

    mine_of = [piece[owner(0), rows_half * t : rows_half * (t + 1), :] for t in range(2)]
    for t in range(2):
        for d in both:
            mine_of[t] = mine_of[t] + take_sum(d, 1, t)
    for t in range(2):
        for d in both:
            mine_of[t] = mine_of[t] + take_sum(d, 2, t)
        out[rows_half * t : rows_half * (t + 1), :] = mine_of[t].astype(jnp.bfloat16)

    for d in both:
        r_copy(d, 4, d).wait_send()
        for away in (3, 1, 2):
            for t in range(2):
                r_copy(d, away, t).wait_send()


def solution(mesh):
    planes = mesh.shape["ctx"] // 4
    ys = mesh.shape["head"] // 2

    def on_device(q_nope, q_rope, latent, key_rope, chosen, w_uk, w_uv, w_out):
        heads = w_uk.shape[0]
        tokens = q_nope.shape[0]
        rows = heads * tokens
        anywhere = pl.BlockSpec(memory_space=pl.ANY)
        dma = pltpu.SemaphoreType.DMA

        def kernel(*refs):
            gather_attend(heads, planes, ys, *refs)

        depth = heads * VHEAD
        width = w_out.shape[1] // 2
        cut = width // ys
        return pl.pallas_call(
            kernel,
            out_shape=jax.ShapeDtypeStruct((cut, tokens), jnp.bfloat16),
            in_specs=[anywhere] * 8,
            out_specs=pl.BlockSpec(memory_space=pltpu.VMEM),
            scratch_shapes=[
                pltpu.VMEM((planes * 4, ROWS, LAT), jnp.bfloat16),
                pltpu.VMEM(q_nope.shape, jnp.bfloat16),
                pltpu.VMEM(q_rope.shape, jnp.bfloat16),
                pltpu.VMEM(w_uk.shape, jnp.bfloat16),
                pltpu.VMEM(w_uv.shape, jnp.bfloat16),
                pltpu.VMEM((rows, LAT), jnp.bfloat16),
                pltpu.VMEM((rows, ROPE), jnp.bfloat16),
                pltpu.VMEM((planes * 4, BLOCK), jnp.float32),
                pltpu.VMEM((rows, 128), jnp.float32),
                pltpu.VMEM((rows, 128), jnp.float32),
                pltpu.VMEM((rows, LAT), jnp.float32),
                dma((11,)),
                dma((3,)),
                dma((3,)),
                dma((1,)),
                dma((1,)),
                dma((3,)),
                dma((3,)),
            ]
            + [dma((2, 4, 3))] * 8
            + [
                pltpu.VMEM((depth, width), jnp.bfloat16),
                pltpu.VMEM((depth, width), jnp.bfloat16),
                pltpu.VMEM((2, width, depth), jnp.bfloat16),
                pltpu.VMEM((tokens, depth), jnp.bfloat16),
                pltpu.VMEM((tokens, depth), jnp.bfloat16),
                pltpu.VMEM((ys, cut, tokens), jnp.float32),
                pltpu.VMEM((2, 7, cut // 2, tokens), jnp.bfloat16),
                pltpu.VMEM((2, 7, cut // 2, tokens), jnp.bfloat16),
                dma((4,)),
                dma((4,)),
                dma((heads,)),
                dma((heads,)),
                dma((2, 7)),
                dma((2, 7)),
                pltpu.SMEM(chosen.shape, jnp.int32),
            ],
            compiler_params=pltpu.CompilerParams(
                collective_id=0, has_side_effects=True, vmem_limit_bytes=67043328
            ),
        )(q_nope, q_rope, latent, key_rope, chosen, w_uk, w_uv, w_out).T

    return jax.shard_map(
        on_device,
        mesh=mesh,
        in_specs=(
            P("ctx", "head"),
            P("ctx", "head"),
            P("ctx", None, None),
            P("ctx", None, None),
            P("ctx", None),
            P("head", None, None),
            P("head", None, None),
            P("head", None),
        ),
        out_specs=P("ctx", "head"),
        check_vma=False,
    )
```
